32 devices in a mesh: grp: 4 (over y, x), band: 8 (over z, core).
Axes of the slice: x: 2, y: 2, z: 4, core: 2. Of those that a mesh axis runs over, the one named last changes fastest.
Arguments:
- probes: bfloat16 [32, 1, 4320, 128], P(('grp', 'band')), may hold values from -6 to 6
- kernel: bfloat16 [32, 5, 1, 289], P(('grp', 'band')), may hold values from -0.375 to 0.375
- pair_station: int32 [32, 5], P(('grp', 'band')), may hold values from 0 to 7, as said below
- pair_count: int32 [32], P(('grp', 'band')), may hold values from 1 to 5, as said below
Outputs:
- basis: float32 [32, 4320, 128], P('grp', 'band')
The draws below stay inside these ranges and needn't reach their ends.
Inputs may be any that keep to these rules, and one draw needn't show every extreme that they name: `pair_station`: slot 0 of source row r names the station row r mod 8; every other slot names a station row within 3 of it, counted cyclically within the super-band. `pair_count`: rows nearer either end of the latitude range tend to use more pair slots.
All inputs are finite; a program needn't handle non-finite values.
Results may differ from the reference program's by a relative error of at most 0.003.
Values may be sent and summed in bfloat16 or wider, within the bound.
No kernel may reach another device: no remote copies, remote signals or barrier semaphores. Data moves between devices by JAX's collectives and lax.ppermute only.
A program may use at most 128 MiB of HBM per device.

```python
import jax
import jax.numpy as jnp
import numpy as np
from jax import lax

L = 4320
P_SIZE = 128
LB = 144
FOOT = 5
LAYERS = 1
ROWS = 32
N_GRP = 4
N_BAND = 8


def draw_pair_station(key, part):
    offsets = jax.random.randint(key, (ROWS, FOOT), -3, 4)
    offsets = offsets.at[:, 0].set(0)
    own_row = jnp.arange(ROWS, dtype=jnp.int32) % N_BAND
    return ((own_row[:, None] + offsets + 4 * N_BAND) % N_BAND).astype(jnp.int32)


def draw_pair_count(key, part):
    row_ids = jnp.arange(ROWS, dtype=jnp.int32)
    distance = jnp.abs(2 * row_ids - (ROWS - 1))
    base_count = 1 + (FOOT - 1) * distance // (ROWS - 1)
    jitter = jax.random.randint(key, (ROWS,), -1, 2)
    result = jnp.clip(base_count + jitter, 1, FOOT)
    result = jnp.where(row_ids == 0, FOOT, result)
    result = jnp.where(row_ids == ROWS // 2, 1, result)
    return result.astype(jnp.int32)


def block_levels(own_key, shape, shards, low, top_value):
    def one(position, parts):
        draws = jax.random.uniform(jax.random.fold_in(jax.random.fold_in(own_key, 6), position), (parts,), jnp.float32, low / len(shards), top_value / len(shards))
        return jnp.repeat(jnp.exp(draws), shape[position] // parts).reshape((-1,) + (1,) * (len(shape) - position - 1))

    level = one(*shards[0])
    for cut in shards[1:]:
        level = level * one(*cut)
    return level


def scatter_about(own_key, shape, spread, bound, pieces=(), kind=jnp.bfloat16):
    entries = jax.random.normal(own_key, shape, jnp.float32) * spread
    if len(pieces) > 0:
        entries = block_levels(own_key, shape, pieces, -0.22, 0.18) * entries
    return jnp.clip(entries, min=-bound, max=bound).astype(kind)


def setup_inputs(seed: int = 0) -> dict:
    streams_of = jax.random.split(jax.random.key(seed), 5)
    return {
        "probes": scatter_about(streams_of[0], (ROWS, LAYERS, L, P_SIZE), 1.0, 6.0, ((0, 32),)),
        "kernel": scatter_about(streams_of[1], (ROWS, FOOT, LAYERS, 2 * LB + 1), (LAYERS * (2 * LB + 1)) ** -0.5, 0.375, ((0, 32),)),
        "pair_station": draw_pair_station(jax.random.fold_in(streams_of[4], 71), 0),
        "pair_count": draw_pair_count(jax.random.fold_in(streams_of[4], 71), 0),
    }


def reference(probes, kernel, pair_station, pair_count):
    lag_index = np.array([(LB - j) % L for j in range(2 * LB + 1)], dtype=np.int32)
    probes_g = probes.reshape(N_GRP, N_BAND, LAYERS, L, P_SIZE)
    kernel_g = kernel.reshape(N_GRP, N_BAND, FOOT, LAYERS, 2 * LB + 1)
    station_g = pair_station.reshape(N_GRP, N_BAND, FOOT)
    count_g = pair_count.reshape(N_GRP, N_BAND)
    station_ids = jnp.arange(N_BAND, dtype=jnp.int32)
    slot_ids = jnp.arange(FOOT, dtype=jnp.int32)

    def group_field(items):
        group_probes, group_kernel, group_station, group_count = items

        def row_step(accum, row_items):
            source, taps, stations, live_pairs = row_items
            spectrum = jnp.fft.rfft(source.astype(jnp.float32), axis=1)
            filters = jnp.zeros((FOOT, LAYERS, L), jnp.float32).at[:, :, lag_index].set(taps.astype(jnp.float32))
            filter_spec = jnp.fft.rfft(filters, axis=2)
            combined = jnp.einsum('flw,lwp->fwp', filter_spec, spectrum)
            partial_value = jnp.fft.irfft(combined, n=L, axis=1).astype(jnp.float32)
            partial_value = lax.optimization_barrier(partial_value.astype(jnp.bfloat16)).astype(jnp.float32)
            live_mask = (slot_ids < live_pairs).astype(jnp.float32)
            picker = (stations[:, None] == station_ids[None, :]).astype(jnp.float32) * live_mask[:, None]
            accum = accum + jnp.einsum('ft,fap->tap', picker, partial_value, precision=lax.Precision.HIGHEST)
            return (accum, None)
        start = jnp.zeros((N_BAND, L, P_SIZE), jnp.float32)
        result, _ = lax.scan(row_step, start, (group_probes, group_kernel, group_station, group_count))
        return result
    field = lax.map(group_field, (probes_g, kernel_g, station_g, count_g))
    flat_field = field.reshape(N_GRP * N_BAND * L, P_SIZE)
    gram = lax.dot_general(flat_field.astype(jnp.float32), flat_field.astype(jnp.float32), (((0,), (0,)), ((), ())), precision=lax.Precision.HIGHEST, preferred_element_type=jnp.float32)
    factor_low = jnp.linalg.cholesky(gram)
    identity = jnp.eye(P_SIZE, dtype=jnp.float32)
    inverse = lax.linalg.triangular_solve(factor_low, identity, left_side=True, lower=True)
    basis = lax.dot_general(flat_field.astype(jnp.float32), inverse.astype(jnp.float32), (((1,), (1,)), ((), ())), precision=lax.Precision.HIGHEST, preferred_element_type=jnp.float32)
    basis = basis * jnp.sqrt(jnp.float32(N_GRP * N_BAND * L))
    return basis.reshape(N_GRP * N_BAND, L, P_SIZE)
```

```python
import functools

import jax
import jax.numpy as jnp
from jax import lax
from jax.experimental import pallas as pl
from jax.experimental.pallas import tpu as pltpu
from jax.sharding import PartitionSpec as P

LANES = 128
TILE = 16
BLOCK = 144


def up(value, step):
    return -(-value // step) * step


def swapped(value, axis, mask):
    pairs = [(source, source ^ mask) for source in range(lax.axis_size(axis))]
    return lax.ppermute(value, axis, pairs)


class Plan:
    def __init__(self, length, taps, slots, band_size):
        self.length, self.taps, self.slots, self.band = length, taps, slots, band_size
        self.half = (taps - 1) // 2
        self.segment = length // band_size
        starts = [b * self.segment - self.half for b in range(band_size)]
        self.aligned = [s // TILE * TILE for s in starts]
        self.shifts = [s - a for s, a in zip(starts, self.aligned)]
        self.rows = up(self.segment, TILE)
        blocks = -(-self.segment // BLOCK)
        self.block_starts = [min(i * BLOCK, self.rows - BLOCK) for i in range(blocks)]
        self.depth = up(BLOCK + taps - 1 + max(self.shifts), TILE)
        self.sub = self.block_starts[-1] + self.depth
        self.chip_starts = [self.aligned[b // 2 * 2] for b in range(band_size)]
        self.offsets = [a - c for a, c in zip(self.aligned, self.chip_starts)]
        self.window = up(max(o + self.sub for o in self.offsets), TILE)
        self.left = -min(self.chip_starts)
        self.right = up(max(max(self.chip_starts) + self.window - length, TILE), TILE)
        self.tap_rows = -(-taps // LANES)
        self.extra = up(slots * self.tap_rows + 1, TILE)
        self.message = self.window + self.extra


def pack_kernel(plan, starts_ref, station_ref, count_ref, taps_ref, probes_ref, *rest):
    peers = len(rest) - 5
    messages = rest[:peers]
    held, rows_f32, rows_bf, in_sems, out_sems = rest[peers:]
    length, left, right = plan.length, plan.left, plan.right
    loads = [
        pltpu.make_async_copy(
            probes_ref.at[pl.ds(0, length)], held.at[pl.ds(left, length)], in_sems.at[0]
        ),
        pltpu.make_async_copy(
            probes_ref.at[pl.ds(length - left, left)], held.at[pl.ds(0, left)], in_sems.at[1]
        ),
        pltpu.make_async_copy(
            probes_ref.at[pl.ds(0, right)], held.at[pl.ds(left + length, right)], in_sems.at[2]
        ),
    ]
    for copy in loads:
        copy.start()
    rows_f32[...] = jnp.zeros_like(rows_f32)
    live = count_ref[0]
    for slot in range(plan.slots):
        keep = (slot < live).astype(jnp.float32)
        for part in range(plan.tap_rows):
            low = part * LANES
            width = min(LANES, plan.taps - low)
            piece = taps_ref[pl.ds(slot, 1), pl.ds(low, width)].astype(jnp.float32)
            rows_f32[pl.ds(slot * plan.tap_rows + part, 1), pl.ds(0, width)] = piece * keep
    lane = lax.broadcasted_iota(jnp.int32, (1, LANES), 1)
    names = jnp.zeros((1, LANES), jnp.float32)
    for slot in range(plan.slots):
        names = jnp.where(lane == slot, station_ref[0, slot].astype(jnp.float32), names)
    rows_f32[pl.ds(plan.slots * plan.tap_rows, 1), :] = names
    rows_bf[...] = rows_f32[...].astype(jnp.bfloat16)
    for copy in loads:
        copy.wait()
    stores = []
    for peer in range(peers):
        start = pl.multiple_of(starts_ref[peer], TILE)
        stores.append(
            pltpu.make_async_copy(
                held.at[pl.ds(start, plan.window)],
                messages[peer].at[pl.ds(0, plan.window)],
                out_sems.at[2 * peer],
            )
        )
        stores.append(
            pltpu.make_async_copy(
                rows_bf, messages[peer].at[pl.ds(plan.window, plan.extra)], out_sems.at[2 * peer + 1]
            )
        )
    for copy in stores:
        copy.start()
    for copy in stores:
        copy.wait()


def pack(plan, probes, taps, station, count, peer_starts):
    peers = plan.band // 2
    smem = pl.BlockSpec(memory_space=pltpu.SMEM)
    return pl.pallas_call(
        functools.partial(pack_kernel, plan),
        out_shape=[jax.ShapeDtypeStruct((plan.message, LANES), jnp.bfloat16)] * peers,
        in_specs=[smem, smem, smem, pl.BlockSpec(memory_space=pltpu.VMEM), pl.BlockSpec(memory_space=pl.ANY)],
        out_specs=[pl.BlockSpec(memory_space=pl.ANY)] * peers,
        scratch_shapes=[
            pltpu.VMEM((plan.left + plan.length + plan.right, LANES), jnp.bfloat16),
            pltpu.VMEM((plan.extra, LANES), jnp.float32),
            pltpu.VMEM((plan.extra, LANES), jnp.bfloat16),
            pltpu.SemaphoreType.DMA((3,)),
            pltpu.SemaphoreType.DMA((2 * peers,)),
        ],
        compiler_params=pltpu.CompilerParams(vmem_limit_bytes=32 << 20),
        cost_estimate=pl.CostEstimate(flops=0, bytes_accessed=4 << 20, transcendentals=0),
        name="pack_windows",
    )(peer_starts, station, count, taps, probes)


def field_kernel(plan, place_ref, *rest):
    messages = rest[: plan.band]
    split_ref, gram_ref, held, field, table, sems = rest[plan.band :]
    offset = pl.multiple_of(place_ref[0], TILE)
    shift = place_ref[1]
    copies = []
    for source in range(plan.band):
        copies.append(
            pltpu.make_async_copy(
                messages[source].at[pl.ds(offset, plan.sub)],
                held.at[source, pl.ds(0, plan.sub)],
                sems.at[source, 0],
            )
        )
        copies.append(
            pltpu.make_async_copy(
                messages[source].at[pl.ds(plan.window, plan.extra)],
                held.at[source, pl.ds(plan.sub, plan.extra)],
                sems.at[source, 1],
            )
        )
    for copy in copies:
        copy.start()
    field[...] = jnp.zeros_like(field)
    lanes = up(plan.depth, LANES)
    for copy in copies:
        copy.wait()

    @pl.loop(0, plan.band)
    def _(source):
        rows = held[source, pl.ds(plan.sub, plan.extra), :].astype(jnp.float32)
        names = rows[plan.slots * plan.tap_rows : plan.slots * plan.tap_rows + 1, :]
        for slot in range(plan.slots):
            pieces = [
                rows[slot * plan.tap_rows + part : slot * plan.tap_rows + part + 1, :]
                for part in range(plan.tap_rows)
            ]
            pieces += [jnp.zeros((1, LANES), jnp.float32)] * (lanes // LANES - plan.tap_rows)
            moved = pltpu.roll(jnp.concatenate(pieces, axis=1), shift, 1)
            spread = jnp.broadcast_to(moved, (BLOCK, lanes))
            rolled = pltpu.roll(spread, 0, 1, stride=1, stride_axis=0)
            table[pl.ds(slot * BLOCK, BLOCK), :] = rolled[:, : plan.depth].astype(jnp.bfloat16)
        right = jnp.concatenate(
            [held[source, pl.ds(start, plan.depth), :] for start in plan.block_starts], axis=1
        )
        for slot in range(plan.slots):
            product = jnp.dot(
                table[pl.ds(slot * BLOCK, BLOCK), :], right, preferred_element_type=jnp.float32
            )
            station = names[0, slot].astype(jnp.int32)
            done = 0
            for i, start in enumerate(plan.block_starts):
                skip = done - start
                field[station, pl.ds(done, BLOCK - skip), :] += product[
                    skip:, i * LANES : (i + 1) * LANES
                ]
                done = start + BLOCK

    gram_ref[...] = jnp.zeros_like(gram_ref)
    inside = lax.broadcasted_iota(jnp.int32, (plan.rows, LANES), 0) < plan.segment

    @pl.loop(0, plan.band)
    def _(station):
        values = jnp.where(inside, field[station], 0.0)
        high = values.astype(jnp.bfloat16)
        low = (values - high.astype(jnp.float32)).astype(jnp.bfloat16)
        both = jnp.concatenate([high, low], axis=1)
        split_ref[station] = both
        square = lax.dot_general(
            both, both, (((0,), (0,)), ((), ())), preferred_element_type=jnp.float32
        )
        gram_ref[...] += (
            square[:LANES, :LANES]
            + square[:LANES, LANES:]
            + square[LANES:, :LANES]
            + square[LANES:, LANES:]
        )


def make_field(plan, place, messages):
    return pl.pallas_call(
        functools.partial(field_kernel, plan),
        out_shape=[
            jax.ShapeDtypeStruct((plan.band, plan.rows, 2 * LANES), jnp.bfloat16),
            jax.ShapeDtypeStruct((LANES, LANES), jnp.float32),
        ],
        in_specs=[pl.BlockSpec(memory_space=pltpu.SMEM)] + [pl.BlockSpec(memory_space=pl.ANY)] * plan.band,
        out_specs=[pl.BlockSpec(memory_space=pltpu.VMEM)] * 2,
        scratch_shapes=[
            pltpu.VMEM((plan.band, plan.sub + plan.extra, LANES), jnp.bfloat16),
            pltpu.VMEM((plan.band, plan.rows, LANES), jnp.float32),
            pltpu.VMEM((plan.slots * BLOCK, plan.depth), jnp.bfloat16),
            pltpu.SemaphoreType.DMA((plan.band, 2)),
        ],
        compiler_params=pltpu.CompilerParams(vmem_limit_bytes=40 << 20),
        cost_estimate=pl.CostEstimate(flops=3 << 30, bytes_accessed=6 << 20, transcendentals=0),
        name="field_and_gram",
    )(place, *messages)


def basis_kernel(segment, weight_ref, split_ref, out_ref):
    weight = weight_ref[...]
    high = weight.astype(jnp.bfloat16)
    low = (weight - high.astype(jnp.float32)).astype(jnp.bfloat16)
    both = jnp.concatenate([high, low], axis=1)
    right = jnp.concatenate([both, both], axis=0)
    product = jnp.dot(split_ref[0], right, preferred_element_type=jnp.float32)
    out_ref[0] = (product[:, :LANES] + product[:, LANES:])[:segment]


def make_basis(plan, weight, split):
    return pl.pallas_call(
        functools.partial(basis_kernel, plan.segment),
        grid=(plan.band,),
        out_shape=jax.ShapeDtypeStruct((plan.band, plan.segment, LANES), jnp.float32),
        in_specs=[
            pl.BlockSpec((LANES, LANES), lambda t: (0, 0)),
            pl.BlockSpec((1, plan.rows, 2 * LANES), lambda t: (t, 0, 0)),
        ],
        out_specs=pl.BlockSpec((1, plan.segment, LANES), lambda t: (t, 0, 0)),
        compiler_params=pltpu.CompilerParams(vmem_limit_bytes=32 << 20),
        name="basis",
    )(weight, split)


def sum_over(value, axis, first_bit=0):
    bits = lax.axis_size(axis).bit_length() - 1
    for bit in range(first_bit, bits):
        value = value + swapped(value, axis, 1 << bit)
    return value


def local(probes, kernel, pair_station, pair_count):
    length, probe_count = probes.shape[2:]
    slots, taps = kernel.shape[1], kernel.shape[3]
    band_size = lax.axis_size("band")
    plan = Plan(length, taps, slots, band_size)
    band = lax.axis_index("band")
    chip_starts = jnp.array(plan.chip_starts, jnp.int32)
    peers = band_size // 2
    peer_starts = jnp.stack([chip_starts[band ^ (2 * k)] for k in range(peers)]) + plan.left
    place = jnp.stack(
        [jnp.array(plan.offsets, jnp.int32)[band], jnp.array(plan.shifts, jnp.int32)[band]]
    )
    messages = pack(
        plan, probes.reshape(length, probe_count), kernel.reshape(slots, taps), pair_station, pair_count, peer_starts
    )
    held = [messages[0]] + [swapped(messages[k], "band", 2 * k) for k in range(1, peers)]
    held = held + [swapped(value, "band", 1) for value in held]
    split, gram = make_field(plan, place, held)
    gram = sum_over(gram, "band")
    gram = sum_over(gram, "grp")
    factor_low = jnp.linalg.cholesky(gram)
    identity = jnp.eye(probe_count, dtype=jnp.float32)
    inverse = lax.linalg.triangular_solve(factor_low, identity, left_side=True, lower=True)
    total_cells = lax.axis_size("grp") * band_size * length
    weight = inverse.T * jnp.sqrt(jnp.float32(total_cells))
    return make_basis(plan, weight, split)


def solution(mesh):
    placed = (
        P(("grp", "band"), None, None, None),
        P(("grp", "band"), None, None, None),
        P(("grp", "band"), None),
        P(("grp", "band")),
    )
    return jax.shard_map(
        local, mesh=mesh, in_specs=placed, out_specs=P("grp", "band", None), check_vma=False
    )
```

```python
import functools

import jax
import jax.numpy as jnp
from jax import lax
from jax.experimental import pallas as pl
from jax.experimental.pallas import tpu as pltpu
from jax.sharding import PartitionSpec as P

LANES = 128
TILE = 16
BLOCK = 144


def up(value, step):
    return -(-value // step) * step


def swapped(value, axis, mask):
    pairs = [(source, source ^ mask) for source in range(lax.axis_size(axis))]
    return lax.ppermute(value, axis, pairs)


class Plan:
    def __init__(self, length, taps, slots, band_size):
        self.length, self.taps, self.slots, self.band = length, taps, slots, band_size
        self.half = (taps - 1) // 2
        self.segment = length // band_size
        starts = [b * self.segment - self.half for b in range(band_size)]
        self.aligned = [s // TILE * TILE for s in starts]
        self.shifts = [s - a for s, a in zip(starts, self.aligned)]
        self.rows = up(self.segment, TILE)
        blocks = -(-self.segment // BLOCK)
        self.block_starts = [min(i * BLOCK, self.rows - BLOCK) for i in range(blocks)]
        self.depth = up(BLOCK + taps - 1 + max(self.shifts), TILE)
        self.sub = self.block_starts[-1] + self.depth
        self.chip_starts = [self.aligned[b // 2 * 2] for b in range(band_size)]
        self.offsets = [a - c for a, c in zip(self.aligned, self.chip_starts)]
        self.window = up(max(o + self.sub for o in self.offsets), TILE)
        self.left = -min(self.chip_starts)
        self.right = up(max(max(self.chip_starts) + self.window - length, TILE), TILE)
        self.tap_rows = -(-taps // LANES)
        self.extra = up(slots * self.tap_rows + 1, TILE)
        self.message = self.window + self.extra


def pack_kernel(plan, band_hbm, station_hbm, count_hbm, taps_hbm, probes_hbm, *rest):
    peers = plan.band // 2
    messages = rest[:peers]
    band_ref, station_ref, count_ref, taps_ref, held, rows_f32, rows_bf, in_sems, out_sems = rest[peers:]
    length, left, right = plan.length, plan.left, plan.right
    loads = [
        (probes_hbm.at[pl.ds(0, length)], held.at[pl.ds(left, length)]),
        (probes_hbm.at[pl.ds(length - left, left)], held.at[pl.ds(0, left)]),
        (probes_hbm.at[pl.ds(0, right)], held.at[pl.ds(left + length, right)]),
        (band_hbm, band_ref),
        (station_hbm, station_ref),
        (count_hbm, count_ref),
        (taps_hbm, taps_ref),
    ]
    loads = [pltpu.make_async_copy(a, b, in_sems.at[i]) for i, (a, b) in enumerate(loads)]
    for copy in loads:
        copy.start()
    rows_f32[...] = jnp.zeros_like(rows_f32)
    for copy in loads[3:]:
        copy.wait()
    live = count_ref[0]
    for slot in range(plan.slots):
        keep = (slot < live).astype(jnp.float32)
        for part in range(plan.tap_rows):
            low = part * LANES
            width = min(LANES, plan.taps - low)
            piece = taps_ref[pl.ds(slot, 1), pl.ds(low, width)].astype(jnp.float32)
            rows_f32[pl.ds(slot * plan.tap_rows + part, 1), pl.ds(0, width)] = piece * keep
    lane = lax.broadcasted_iota(jnp.int32, (1, LANES), 1)
    names = jnp.zeros((1, LANES), jnp.float32)
    for slot in range(plan.slots):
        names = jnp.where(lane == slot, station_ref[0, slot].astype(jnp.float32), names)
    rows_f32[pl.ds(plan.slots * plan.tap_rows, 1), :] = names
    rows_bf[...] = rows_f32[...].astype(jnp.bfloat16)
    for copy in loads[:3]:
        copy.wait()
    band = band_ref[0]
    stores = []
    for peer in range(peers):
        chip = (band ^ (2 * peer)) // 2
        start = pl.multiple_of((chip * (2 * plan.segment) + left - plan.half) // TILE * TILE, TILE)
        stores.append(
            pltpu.make_async_copy(
                held.at[pl.ds(start, plan.window)],
                messages[peer].at[pl.ds(0, plan.window)],
                out_sems.at[2 * peer],
            )
        )
        stores.append(
            pltpu.make_async_copy(
                rows_bf, messages[peer].at[pl.ds(plan.window, plan.extra)], out_sems.at[2 * peer + 1]
            )
        )
    for copy in stores:
        copy.start()
    for copy in stores:
        copy.wait()


def pack(plan, band, probes, taps, station, count):
    peers = plan.band // 2
    hbm = pl.BlockSpec(memory_space=pltpu.HBM)
    return pl.pallas_call(
        functools.partial(pack_kernel, plan),
        out_shape=[jax.ShapeDtypeStruct((plan.message, LANES), jnp.bfloat16)] * peers,
        in_specs=[hbm] * 5,
        out_specs=[pl.BlockSpec(memory_space=pl.ANY)] * peers,
        scratch_shapes=[
            pltpu.SMEM((1,), jnp.int32),
            pltpu.SMEM(station.shape, jnp.int32),
            pltpu.SMEM((1,), jnp.int32),
            pltpu.VMEM(taps.shape, jnp.bfloat16),
            pltpu.VMEM((plan.left + plan.length + plan.right, LANES), jnp.bfloat16),
            pltpu.VMEM((plan.extra, LANES), jnp.float32),
            pltpu.VMEM((plan.extra, LANES), jnp.bfloat16),
            pltpu.SemaphoreType.DMA((7,)),
            pltpu.SemaphoreType.DMA((2 * peers,)),
        ],
        compiler_params=pltpu.CompilerParams(vmem_limit_bytes=60 << 20),
        cost_estimate=pl.CostEstimate(flops=0, bytes_accessed=4 << 20, transcendentals=0),
        name="pack_windows",
    )(band, station, count, taps, probes)


def add_products(plan, place, messages, field, table):
    offset, shift = place
    lanes = up(plan.depth, LANES)
    for source, message in enumerate(messages):
        rows = message[pl.ds(plan.window, plan.extra), :].astype(jnp.float32)
        names = rows[plan.slots * plan.tap_rows : plan.slots * plan.tap_rows + 1, :]
        for slot in range(plan.slots):
            pieces = [
                rows[slot * plan.tap_rows + part : slot * plan.tap_rows + part + 1, :]
                for part in range(plan.tap_rows)
            ]
            pieces += [jnp.zeros((1, LANES), jnp.float32)] * (lanes // LANES - plan.tap_rows)
            moved = pltpu.roll(jnp.concatenate(pieces, axis=1), shift, 1)
            spread = jnp.broadcast_to(moved, (BLOCK, lanes))
            rolled = pltpu.roll(spread, 0, 1, stride=1, stride_axis=0)
            table[source, pl.ds(slot * BLOCK, BLOCK), :] = rolled[:, : plan.depth].astype(jnp.bfloat16)
        right = jnp.concatenate(
            [
                message[pl.ds(pl.multiple_of(offset + start, TILE), plan.depth), :]
                for start in plan.block_starts
            ],
            axis=1,
        )
        for slot in range(plan.slots):
            product = jnp.dot(
                table[source, pl.ds(slot * BLOCK, BLOCK), :], right, preferred_element_type=jnp.float32
            )
            station = names[0, slot].astype(jnp.int32)
            done = 0
            for i, start in enumerate(plan.block_starts):
                skip = done - start
                field[station, pl.ds(done, BLOCK - skip), :] += product[
                    skip:, i * LANES : (i + 1) * LANES
                ]
                done = start + BLOCK


def split_and_gram(plan, field, split_ref, gram_ref):
    gram_ref[...] = jnp.zeros_like(gram_ref)
    inside = lax.broadcasted_iota(jnp.int32, (plan.rows, LANES), 0) < plan.segment

    @pl.loop(0, plan.band)
    def _(station):
        values = jnp.where(inside, field[station], 0.0)
        high = values.astype(jnp.bfloat16)
        low = (values - high.astype(jnp.float32)).astype(jnp.bfloat16)
        both = jnp.concatenate([high, low], axis=1)
        split_ref[station] = both
        square = lax.dot_general(
            both, both, (((0,), (0,)), ((), ())), preferred_element_type=jnp.float32
        )
        gram_ref[...] += (
            square[:LANES, :LANES]
            + square[:LANES, LANES:]
            + square[LANES:, :LANES]
            + square[LANES:, LANES:]
        )


def field_kernel(plan, first, last, count, band_ref, *rest):
    messages, rest = rest[:count], rest[count:]
    if not first:
        field, rest = rest[0], rest[1:]
    base = band_ref[0] * plan.segment + plan.left - plan.half
    chip = band_ref[0] // 2 * (2 * plan.segment) + plan.left - plan.half
    aligned = base // TILE * TILE
    place = (aligned - chip // TILE * TILE, base - aligned)
    if last:
        split_ref, gram_ref, table = rest
        add_products(plan, place, messages, field, table)
        split_and_gram(plan, field, split_ref, gram_ref)
    else:
        out_ref, table = rest
        if first:
            out_ref[...] = jnp.zeros_like(out_ref)
        add_products(plan, place, messages, out_ref, table)


def add_rows(plan, band, messages, field, last):
    count, first = len(messages), field is None
    vmem = pl.BlockSpec(memory_space=pltpu.VMEM)
    field_shape = jax.ShapeDtypeStruct((plan.band, plan.rows, LANES), jnp.float32)
    if last:
        out_shape = [
            jax.ShapeDtypeStruct((plan.band, plan.rows, 2 * LANES), jnp.bfloat16),
            jax.ShapeDtypeStruct((LANES, LANES), jnp.float32),
        ]
    else:
        out_shape = field_shape
    operands = [band, *messages] + ([] if first else [field])
    return pl.pallas_call(
        functools.partial(field_kernel, plan, first, last, count),
        out_shape=out_shape,
        in_specs=[pl.BlockSpec(memory_space=pltpu.SMEM)] + [vmem] * (len(operands) - 1),
        out_specs=[vmem] * 2 if last else vmem,
        input_output_aliases={} if first or last else {len(operands) - 1: 0},
        scratch_shapes=[pltpu.VMEM((count, plan.slots * BLOCK, plan.depth), jnp.bfloat16)],
        compiler_params=pltpu.CompilerParams(vmem_limit_bytes=24 << 20),
        cost_estimate=pl.CostEstimate(flops=3 << 30, bytes_accessed=6 << 20, transcendentals=0),
        name="field_and_gram" if last else "field",
    )(*operands)


def basis_kernel(plan, weight_ref, split_ref, out_ref):
    weight = weight_ref[...]
    high = weight.astype(jnp.bfloat16)
    low = (weight - high.astype(jnp.float32)).astype(jnp.bfloat16)
    both = jnp.concatenate([high, low], axis=1)
    right = jnp.concatenate([both, both], axis=0)
    for station in range(plan.band):
        product = jnp.dot(split_ref[station], right, preferred_element_type=jnp.float32)
        total = product[:, :LANES] + product[:, LANES:]
        out_ref[pl.ds(station, plan.segment, stride=plan.band), :] = total[: plan.segment]


def make_basis(plan, weight, split):
    vmem = pl.BlockSpec(memory_space=pltpu.VMEM)
    rows = pl.pallas_call(
        functools.partial(basis_kernel, plan),
        out_shape=jax.ShapeDtypeStruct((plan.segment * plan.band, LANES), jnp.float32),
        in_specs=[vmem, vmem],
        out_specs=vmem,
        compiler_params=pltpu.CompilerParams(vmem_limit_bytes=24 << 20),
        name="basis",
    )(weight, split)
    return rows.reshape(plan.segment, plan.band, LANES).transpose(1, 0, 2)


def sum_four(value, axis, bit):
    return value + sum(swapped(value, axis, k << bit) for k in (1, 2, 3))


def sum_over(value, axis, bits):
    while bits:
        if axis == "grp" and len(bits) > 1:
            value = sum_four(value, axis, bits[0])
            bits = bits[2:]
        else:
            value = value + swapped(value, axis, 1 << bits[0])
            bits = bits[1:]
    return value


def local(probes, kernel, pair_station, pair_count):
    length, probe_count = probes.shape[2:]
    slots, taps = kernel.shape[1], kernel.shape[3]
    band_size, grp_size = lax.axis_size("band"), lax.axis_size("grp")
    plan = Plan(length, taps, slots, band_size)
    band = lax.axis_index("band").astype(jnp.int32).reshape(1)
    messages = pack(
        plan, band, probes.reshape(length, probe_count), kernel.reshape(slots, taps), pair_station, pair_count
    )
    peers = band_size // 2
    arrived = [messages[0]] + [swapped(messages[k], "band", 2 * k) for k in range(1, peers)]
    field = None
    for k, value in enumerate(arrived):
        field = add_rows(plan, band, [value, swapped(value, "band", 1)], field, k == peers - 1)
    split, gram = field
    band_bits, grp_bits = (list(range(n.bit_length() - 1)) for n in (band_size, grp_size))
    gram = sum_over(gram, "band", band_bits[:1])
    gram = sum_over(gram, "grp", grp_bits)
    gram = sum_over(gram, "band", band_bits[1:])
    factor_low = jnp.linalg.cholesky(gram)
    identity = jnp.eye(probe_count, dtype=jnp.float32)
    inverse = lax.linalg.triangular_solve(factor_low, identity, left_side=True, lower=True)
    total_cells = grp_size * band_size * length
    weight = inverse.T * jnp.sqrt(jnp.float32(total_cells))
    return make_basis(plan, weight, split)


def solution(mesh):
    placed = (
        P(("grp", "band"), None, None, None),
        P(("grp", "band"), None, None, None),
        P(("grp", "band"), None),
        P(("grp", "band")),
    )
    return jax.shard_map(
        local, mesh=mesh, in_specs=placed, out_specs=P("grp", "band", None), check_vma=False
    )
```

```python
import functools

import jax
import jax.numpy as jnp
from jax import lax
from jax.experimental import pallas as pl
from jax.experimental.pallas import tpu as pltpu
from jax.sharding import PartitionSpec as P

LANES = 128
TILE = 16
BLOCK = 144
PANEL = 16


def up(value, step):
    return -(-value // step) * step


def swapped(value, axis, mask):
    pairs = [(source, source ^ mask) for source in range(lax.axis_size(axis))]
    return lax.ppermute(value, axis, pairs)


class Plan:
    def __init__(self, length, taps, slots, band_size):
        self.length, self.taps, self.slots, self.band = length, taps, slots, band_size
        self.half = (taps - 1) // 2
        self.segment = length // band_size
        starts = [b * self.segment - self.half for b in range(band_size)]
        self.aligned = [s // TILE * TILE for s in starts]
        self.shifts = [s - a for s, a in zip(starts, self.aligned)]
        self.rows = up(self.segment, TILE)
        blocks = -(-self.segment // BLOCK)
        self.block_starts = [min(i * BLOCK, self.rows - BLOCK) for i in range(blocks)]
        self.depth = up(BLOCK + taps - 1 + max(self.shifts), TILE)
        self.sub = self.block_starts[-1] + self.depth
        self.chip_starts = [self.aligned[b // 2 * 2] for b in range(band_size)]
        self.offsets = [a - c for a, c in zip(self.aligned, self.chip_starts)]
        self.window = up(max(o + self.sub for o in self.offsets), TILE)
        self.left = -min(self.chip_starts)
        self.right = up(max(max(self.chip_starts) + self.window - length, TILE), TILE)
        self.tap_rows = -(-taps // LANES)
        self.extra = up(slots * self.tap_rows + 1, TILE)
        self.whole = self.window + self.extra
        self.near = self.sub + self.extra
        self.sends = [(0, False)] + [(m, True) for m in (2, 3)][: band_size - 2]
        self.sends += [(m, False) for m in range(4, band_size, 2)]

    def size(self, near):
        return self.sub if near else self.window

    def shapes(self):
        return [jax.ShapeDtypeStruct((self.size(near) + self.extra, LANES), jnp.bfloat16) for _, near in self.sends]


def pack_kernel(plan, band_hbm, station_hbm, count_hbm, taps_hbm, probes_hbm, *rest):
    peers = len(plan.sends)
    messages = rest[:peers]
    band_ref, station_ref, count_ref, taps_ref, held, rows_f32, rows_bf, in_sems, out_sems = rest[peers:]
    length, left, right = plan.length, plan.left, plan.right
    loads = [
        (probes_hbm.at[pl.ds(0, length)], held.at[pl.ds(left, length)]),
        (probes_hbm.at[pl.ds(length - left, left)], held.at[pl.ds(0, left)]),
        (probes_hbm.at[pl.ds(0, right)], held.at[pl.ds(left + length, right)]),
        (band_hbm, band_ref),
        (station_hbm, station_ref),
        (count_hbm, count_ref),
        (taps_hbm, taps_ref),
    ]
    loads = [pltpu.make_async_copy(a, b, in_sems.at[i]) for i, (a, b) in enumerate(loads)]
    for copy in loads:
        copy.start()
    rows_f32[...] = jnp.zeros_like(rows_f32)
    for copy in loads[3:]:
        copy.wait()
    live = count_ref[0]
    for slot in range(plan.slots):
        keep = (slot < live).astype(jnp.float32)
        for part in range(plan.tap_rows):
            low = part * LANES
            width = min(LANES, plan.taps - low)
            piece = taps_ref[pl.ds(slot, 1), pl.ds(low, width)].astype(jnp.float32)
            rows_f32[pl.ds(slot * plan.tap_rows + part, 1), pl.ds(0, width)] = piece * keep
    lane = lax.broadcasted_iota(jnp.int32, (1, LANES), 1)
    names = jnp.zeros((1, LANES), jnp.float32)
    for slot in range(plan.slots):
        names = jnp.where(lane == slot, station_ref[0, slot].astype(jnp.float32), names)
    rows_f32[pl.ds(plan.slots * plan.tap_rows, 1), :] = names
    rows_bf[...] = rows_f32[...].astype(jnp.bfloat16)
    for copy in loads[:3]:
        copy.wait()
    band = band_ref[0]
    stores = []
    for peer, (mask, near) in enumerate(plan.sends):
        other = band ^ mask
        if not near:
            other = other // 2 * 2
        start = pl.multiple_of((other * plan.segment + left - plan.half) // TILE * TILE, TILE)
        size = plan.size(near)
        stores.append(
            pltpu.make_async_copy(
                held.at[pl.ds(start, size)],
                messages[peer].at[pl.ds(0, size)],
                out_sems.at[2 * peer],
            )
        )
        stores.append(
            pltpu.make_async_copy(
                rows_bf, messages[peer].at[pl.ds(size, plan.extra)], out_sems.at[2 * peer + 1]
            )
        )
    for copy in stores:
        copy.start()
    for copy in stores:
        copy.wait()


def pack(plan, band, probes, taps, station, count):
    peers = len(plan.sends)
    hbm = pl.BlockSpec(memory_space=pltpu.HBM)
    return pl.pallas_call(
        functools.partial(pack_kernel, plan),
        out_shape=plan.shapes(),
        in_specs=[hbm] * 5,
        out_specs=[pl.BlockSpec(memory_space=pl.ANY)] * peers,
        scratch_shapes=[
            pltpu.SMEM((1,), jnp.int32),
            pltpu.SMEM(station.shape, jnp.int32),
            pltpu.SMEM((1,), jnp.int32),
            pltpu.VMEM(taps.shape, jnp.bfloat16),
            pltpu.VMEM((plan.left + plan.length + plan.right, LANES), jnp.bfloat16),
            pltpu.VMEM((plan.extra, LANES), jnp.float32),
            pltpu.VMEM((plan.extra, LANES), jnp.bfloat16),
            pltpu.SemaphoreType.DMA((7,)),
            pltpu.SemaphoreType.DMA((2 * peers,)),
        ],
        compiler_params=pltpu.CompilerParams(vmem_limit_bytes=60 << 20),
        cost_estimate=pl.CostEstimate(flops=0, bytes_accessed=4 << 20, transcendentals=0),
        name="pack_windows",
    )(band, station, count, taps, probes)


def add_products(plan, place, messages, field, table):
    offset, shift = place
    lanes = up(plan.depth, LANES)
    for source, message in enumerate(messages):
        near = message.shape[0] == plan.near
        source = source % 2
        rows = message[pl.ds(plan.size(near), plan.extra), :].astype(jnp.float32)
        names = rows[plan.slots * plan.tap_rows : plan.slots * plan.tap_rows + 1, :]
        for slot in range(plan.slots):
            pieces = [
                rows[slot * plan.tap_rows + part : slot * plan.tap_rows + part + 1, :]
                for part in range(plan.tap_rows)
            ]
            pieces += [jnp.zeros((1, LANES), jnp.float32)] * (lanes // LANES - plan.tap_rows)
            moved = pltpu.roll(jnp.concatenate(pieces, axis=1), shift, 1)
            spread = jnp.broadcast_to(moved, (BLOCK, lanes))
            rolled = pltpu.roll(spread, 0, 1, stride=1, stride_axis=0)
            table[source, pl.ds(slot * BLOCK, BLOCK), :] = rolled[:, : plan.depth].astype(jnp.bfloat16)
        right = jnp.concatenate(
            [
                message[pl.ds(start if near else pl.multiple_of(offset + start, TILE), plan.depth), :]
                for start in plan.block_starts
            ],
            axis=1,
        )
        for slot in range(plan.slots):
            product = jnp.dot(
                table[source, pl.ds(slot * BLOCK, BLOCK), :], right, preferred_element_type=jnp.float32
            )
            station = names[0, slot].astype(jnp.int32)
            done = 0
            for i, start in enumerate(plan.block_starts):
                skip = done - start
                field[station, pl.ds(done, BLOCK - skip), :] += product[
                    skip:, i * LANES : (i + 1) * LANES
                ]
                done = start + BLOCK


def split_and_gram(plan, field, split_ref, gram_ref, total):
    total[...] = jnp.zeros_like(total)
    inside = lax.broadcasted_iota(jnp.int32, (plan.rows, LANES), 0) < plan.segment

    @pl.loop(0, plan.band)
    def _(station):
        values = jnp.where(inside, field[station], 0.0)
        high = values.astype(jnp.bfloat16)
        low = (values - high.astype(jnp.float32)).astype(jnp.bfloat16)
        both = jnp.concatenate([high, low], axis=1)
        split_ref[station] = both
        total[...] += lax.dot_general(
            both, both, (((0,), (0,)), ((), ())), preferred_element_type=jnp.float32
        )

    rows = total[pl.ds(0, LANES), :] + total[pl.ds(LANES, LANES), :]
    gram_ref[...] = folded(rows[:, :LANES] + rows[:, LANES:])


def field_kernel(plan, first, last, count, band_ref, *rest):
    messages, rest = rest[:count], rest[count:]
    if not first:
        field, rest = rest[0], rest[1:]
    base = band_ref[0] * plan.segment + plan.left - plan.half
    chip = band_ref[0] // 2 * (2 * plan.segment) + plan.left - plan.half
    aligned = base // TILE * TILE
    place = (aligned - chip // TILE * TILE, base - aligned)
    if last:
        split_ref, gram_ref, table, total = rest
        add_products(plan, place, messages, field, table)
        split_and_gram(plan, field, split_ref, gram_ref, total)
    else:
        out_ref, table = rest
        if first:
            out_ref[...] = jnp.zeros_like(out_ref)
        add_products(plan, place, messages, out_ref, table)


def add_rows(plan, band, messages, field, last):
    count, first = len(messages), field is None
    vmem = pl.BlockSpec(memory_space=pltpu.VMEM)
    field_shape = jax.ShapeDtypeStruct((plan.band, plan.rows, LANES), jnp.float32)
    if last:
        out_shape = [
            jax.ShapeDtypeStruct((plan.band, plan.rows, 2 * LANES), jnp.bfloat16),
            jax.ShapeDtypeStruct((LANES * 3 // 4, LANES), jnp.float32),
        ]
    else:
        out_shape = field_shape
    operands = [band, *messages] + ([] if first else [field])
    return pl.pallas_call(
        functools.partial(field_kernel, plan, first, last, count),
        out_shape=out_shape,
        in_specs=[pl.BlockSpec(memory_space=pltpu.SMEM)] + [vmem] * (len(operands) - 1),
        out_specs=[vmem] * 2 if last else vmem,
        input_output_aliases={} if first or last else {len(operands) - 1: 0},
        scratch_shapes=[pltpu.VMEM((min(count, 2), plan.slots * BLOCK, plan.depth), jnp.bfloat16)]
        + ([pltpu.VMEM((2 * LANES, 2 * LANES), jnp.float32)] if last else []),
        compiler_params=pltpu.CompilerParams(vmem_limit_bytes=24 << 20),
        cost_estimate=pl.CostEstimate(flops=1 << 20, bytes_accessed=1 << 16, transcendentals=0),
        name="field_and_gram" if last else "field",
    )(*operands)


def three_parts(value):
    first = value.astype(jnp.bfloat16)
    value = value - first.astype(jnp.float32)
    second = value.astype(jnp.bfloat16)
    return first, second, (value - second.astype(jnp.float32)).astype(jnp.bfloat16)


def invert_factor(gram, left, right):
    size = gram.shape[0]
    row = lax.broadcasted_iota(jnp.int32, (size, size), 0)
    col = lax.broadcasted_iota(jnp.int32, (size, size), 1)
    left[...] = gram
    right[...] = (row == col).astype(jnp.float32)
    sub = lax.broadcasted_iota(jnp.int32, (8, size), 0)
    for base in range(0, size, PANEL):
        x, y = left[pl.ds(base, PANEL), :], right[pl.ds(base, PANEL), :]
        square = {}
        for i in range(PANEL):
            for k in range(i, PANEL):
                square[i, k] = jnp.broadcast_to(x[i : i + 1, base + k : base + k + 1], (8, size))
        xs = [jnp.broadcast_to(x[i : i + 1, :], (8, size)) for i in range(PANEL)]
        ys = [jnp.broadcast_to(y[i : i + 1, :], (8, size)) for i in range(PANEL)]
        for i in range(PANEL):
            scale = lax.rsqrt(square[i, i])
            scaled = {k: square[i, k] * scale for k in range(i + 1, PANEL)}
            xs[i], ys[i] = xs[i] * scale, ys[i] * scale
            for k in range(i + 1, PANEL):
                for m in range(k, PANEL):
                    square[k, m] = square[k, m] - scaled[k] * scaled[m]
                xs[k] = xs[k] - scaled[k] * xs[i]
                ys[k] = ys[k] - scaled[k] * ys[i]
        upper, lower = [], []
        for tile in range(0, PANEL, 8):
            u, v = xs[tile], ys[tile]
            for i in range(1, 8):
                u = jnp.where(sub == i, xs[tile + i], u)
                v = jnp.where(sub == i, ys[tile + i], v)
            upper.append(u)
            lower.append(v)
        u, v = jnp.concatenate(upper, axis=0), jnp.concatenate(lower, axis=0)
        right[pl.ds(base, PANEL), :] = v
        rest = size - base - PANEL
        if rest:
            a, b, c = three_parts(jnp.concatenate([u, v], axis=1))
            one = jnp.concatenate([part[:, :size] for part in (a, a, b, a, b, c)], axis=0)
            two = jnp.concatenate([a, b, a, c, b, a], axis=0)
            update = lax.dot_general(
                one, two, (((0,), (0,)), ((), ())), preferred_element_type=jnp.float32
            )[base + PANEL :]
            left[pl.ds(base + PANEL, rest), :] -= update[:, :size]
            right[pl.ds(base + PANEL, rest), :] -= update[:, size:]


def folded(gram):
    half = LANES // 2
    corner = pltpu.roll(gram[half:, :], half, 1)
    first = lax.broadcasted_iota(jnp.int32, (half // 2, LANES), 1) < half
    joined = jnp.where(first, corner[: half // 2], gram[half + half // 2 :, :])
    return jnp.concatenate([gram[:half], joined], axis=0)


def unfolded(packed):
    half = LANES // 2
    joined = packed[half:]
    return jnp.concatenate([packed[:half], pltpu.roll(joined, half, 1), joined], axis=0)


def basis_kernel(plan, scale, addends, *rest):
    packed = rest[0][...]
    for other in rest[1:addends]:
        packed = packed + other[...]
    split_ref, out_ref, left, right = rest[addends:]
    invert_factor(unfolded(packed), left, right)
    weight = right[...] * scale
    high = weight.astype(jnp.bfloat16)
    low = (weight - high.astype(jnp.float32)).astype(jnp.bfloat16)
    turned = jnp.concatenate(
        [jnp.concatenate([high, high], axis=1), jnp.concatenate([low, low], axis=1)], axis=0
    )
    for station in range(plan.band):
        product = lax.dot_general(
            split_ref[station], turned, (((1,), (1,)), ((), ())), preferred_element_type=jnp.float32
        )
        total = product[:, :LANES] + product[:, LANES:]
        out_ref[pl.ds(station, plan.segment, stride=plan.band), :] = total[: plan.segment]


def make_basis(plan, scale, grams, split):
    vmem = pl.BlockSpec(memory_space=pltpu.VMEM)
    rows = pl.pallas_call(
        functools.partial(basis_kernel, plan, scale, len(grams)),
        out_shape=jax.ShapeDtypeStruct((plan.segment * plan.band, LANES), jnp.float32),
        in_specs=[vmem] * (len(grams) + 1),
        out_specs=vmem,
        scratch_shapes=[pltpu.VMEM((LANES, LANES), jnp.float32)] * 2,
        compiler_params=pltpu.CompilerParams(vmem_limit_bytes=24 << 20),
        name="factor_and_basis",
    )(*grams, split)
    return rows.reshape(plan.segment, plan.band, LANES).transpose(1, 0, 2)


def sum_four(value, axis, bit):
    return value + sum(swapped(value, axis, k << bit) for k in (1, 2, 3))


def sum_over(value, axis, bits):
    while bits:
        if axis == "grp" and len(bits) > 1:
            value = sum_four(value, axis, bits[0])
            bits = bits[2:]
        else:
            value = value + swapped(value, axis, 1 << bits[0])
            bits = bits[1:]
    return value


def both_cores(values):
    return values + [swapped(value, "band", 1) for value in values]


def local(probes, kernel, pair_station, pair_count):
    length, probe_count = probes.shape[2:]
    slots, taps = kernel.shape[1], kernel.shape[3]
    band_size, grp_size = lax.axis_size("band"), lax.axis_size("grp")
    plan = Plan(length, taps, slots, band_size)
    band = lax.axis_index("band").astype(jnp.int32).reshape(1)
    messages = pack(
        plan, band, probes.reshape(length, probe_count), kernel.reshape(slots, taps), pair_station, pair_count
    )
    arrived = [
        value if mask == 0 else swapped(value, "band", mask)
        for value, (mask, near) in zip(messages, plan.sends)
    ]
    near = sum(near for _, near in plan.sends)
    field = add_rows(plan, band, both_cores(arrived[:1]), None, False)
    field = add_rows(plan, band, arrived[1 : 1 + near], field, False)
    rest, field = lax.optimization_barrier((arrived[1 + near :], field))
    field = add_rows(plan, band, both_cores(rest), field, True)
    split, gram = field
    band_bits, grp_bits = (list(range(n.bit_length() - 1)) for n in (band_size, grp_size))
    gram = sum_over(gram, "band", band_bits[:1])
    gram = sum_over(gram, "grp", grp_bits)
    gram = sum_over(gram, "band", band_bits[1:-1])
    grams = [gram, swapped(gram, "band", 1 << band_bits[-1])]
    scale = float(grp_size * band_size * length) ** 0.5
    return make_basis(plan, scale, grams, split)


def solution(mesh):
    placed = (
        P(("grp", "band"), None, None, None),
        P(("grp", "band"), None, None, None),
        P(("grp", "band"), None),
        P(("grp", "band")),
    )
    return jax.shard_map(
        local, mesh=mesh, in_specs=placed, out_specs=P("grp", "band", None), check_vma=False
    )
```

```python
import functools

import jax
import jax.numpy as jnp
from jax import lax
from jax.experimental import pallas as pl
from jax.experimental.pallas import tpu as pltpu
from jax.sharding import PartitionSpec as P

LANES = 128
TILE = 16
BLOCK = 32
PANEL = 16
CHUNK = 192


def up(value, step):
    return -(-value // step) * step


def swapped(value, axis, mask):
    pairs = [(source, source ^ mask) for source in range(lax.axis_size(axis))]
    return lax.ppermute(value, axis, pairs)


class Plan:
    def __init__(self, length, taps, slots, band_size):
        self.length, self.taps, self.slots, self.band = length, taps, slots, band_size
        self.half = (taps - 1) // 2
        self.segment = length // band_size
        starts = [b * self.segment - self.half for b in range(band_size)]
        self.aligned = [s // TILE * TILE for s in starts]
        self.shifts = [s - a for s, a in zip(starts, self.aligned)]
        self.rows = up(self.segment, TILE)
        blocks = -(-self.segment // BLOCK)
        self.block_starts = [min(i * BLOCK, self.rows - BLOCK) for i in range(blocks)]
        self.depth = up(BLOCK + taps - 1 + max(self.shifts), TILE)
        self.sub = self.block_starts[-1] + self.depth
        self.chip_starts = [self.aligned[b // 2 * 2] for b in range(band_size)]
        self.offsets = [a - c for a, c in zip(self.aligned, self.chip_starts)]
        reach = self.segment + taps - 1
        self.window = up(max(o + s + reach for o, s in zip(self.offsets, self.shifts)), TILE)
        self.left = -min(self.chip_starts)
        self.tap_rows = -(-taps // LANES)
        self.extra = up(slots * self.tap_rows + 1, TILE)
        self.whole = self.window + self.extra
        assert max(self.offsets) + self.sub <= self.whole
        self.near = self.sub + self.extra
        self.sends = [(0, False)] + [(m, True) for m in (2, 3)][: band_size - 2]
        self.sends += [(m, False) for m in range(4, band_size, 2)]

    def size(self, near):
        return self.sub if near else self.window

    def shapes(self):
        return [jax.ShapeDtypeStruct((self.size(near) + self.extra, LANES), jnp.bfloat16) for _, near in self.sends]


def pack_kernel(plan, band_ref, count_ref, station_hbm, taps_hbm, probes_hbm, *rest):
    peers = len(plan.sends)
    messages = rest[:peers]
    station_ref, taps_ref, rows_f32, in_sems, out_sems = rest[peers:]
    loads = [(station_hbm, station_ref), (taps_hbm, taps_ref)]
    loads = [pltpu.make_async_copy(a, b, in_sems.at[i]) for i, (a, b) in enumerate(loads)]
    for copy in loads:
        copy.start()

    def windows(peer, act):
        mask, near = plan.sends[peer]
        size = plan.size(near)
        other = band_ref[0] ^ mask
        if not near:
            other = other // 2 * 2
        plain = other >= 0
        for index in range(0, plan.band, 1 if near else 2):
            start = plan.aligned[index]
            if start < 0:
                first, cut = plan.length + start, -start
            elif start + size > plan.length:
                first, cut = start, plan.length - start
            else:
                continue
            plain = jnp.logical_and(plain, other != index)

            @pl.when(other == index)
            def _():
                for piece, (low, to, count) in enumerate([(first, 0, cut), (0, cut, size - cut)]):
                    act(
                        pltpu.make_async_copy(
                            probes_hbm.at[pl.ds(low, count)],
                            messages[peer].at[pl.ds(to, count)],
                            out_sems.at[2 * peer + piece],
                        )
                    )

        @pl.when(plain)
        def _():
            low = (other * plan.segment + plan.left - plan.half) // TILE * TILE - plan.left
            act(
                pltpu.make_async_copy(
                    probes_hbm.at[pl.ds(pl.multiple_of(low, TILE), size)],
                    messages[peer].at[pl.ds(0, size)],
                    out_sems.at[2 * peer],
                )
            )

    order = list(range(peers))[::-1]
    for peer in order:
        windows(peer, lambda copy: copy.start())
    rows_f32[...] = jnp.zeros_like(rows_f32)
    for copy in loads:
        copy.wait()
    live = count_ref[0]
    for slot in range(plan.slots):
        keep = (slot < live).astype(jnp.float32)
        for part in range(plan.tap_rows):
            low = part * LANES
            width = min(LANES, plan.taps - low)
            piece = taps_ref[pl.ds(slot, 1), pl.ds(low, width)].astype(jnp.float32)
            rows_f32[pl.ds(slot * plan.tap_rows + part, 1), pl.ds(0, width)] = piece * keep
    lane = lax.broadcasted_iota(jnp.int32, (1, LANES), 1)
    names = jnp.zeros((1, LANES), jnp.float32)
    for slot in range(plan.slots):
        names = jnp.where(lane == slot, station_ref[0, slot].astype(jnp.float32), names)
    rows_f32[pl.ds(plan.slots * plan.tap_rows, 1), :] = names
    rows_bf = rows_f32[...].astype(jnp.bfloat16)
    for peer in order:
        messages[peer][pl.ds(plan.size(plan.sends[peer][1]), plan.extra), :] = rows_bf
    for peer in order:
        windows(peer, lambda copy: copy.wait())


def stay(value):
    return pltpu.with_memory_space_constraint(value, pltpu.HBM)


def pack(plan, band, probes, taps, station, count):
    peers = len(plan.sends)
    hbm = pl.BlockSpec(memory_space=pltpu.HBM)
    smem = pl.BlockSpec(memory_space=pltpu.SMEM)
    return pl.pallas_call(
        functools.partial(pack_kernel, plan),
        out_shape=plan.shapes(),
        in_specs=[smem] * 2 + [hbm] * 3,
        out_specs=[pl.BlockSpec(memory_space=pltpu.VMEM)] * peers,
        scratch_shapes=[
            pltpu.SMEM(station.shape, jnp.int32),
            pltpu.VMEM(taps.shape, jnp.bfloat16),
            pltpu.VMEM((plan.extra, LANES), jnp.float32),
            pltpu.SemaphoreType.DMA((2,)),
            pltpu.SemaphoreType.DMA((2 * peers,)),
        ],
        compiler_params=pltpu.CompilerParams(vmem_limit_bytes=8 << 20),
        cost_estimate=pl.CostEstimate(flops=0, bytes_accessed=4 << 20, transcendentals=0),
        name="pack_windows",
    )(band, count, stay(station), stay(taps), stay(probes))


def add_products(plan, place, messages, field, table):
    offset, shift = place
    lanes = up(plan.depth, LANES)
    for source, message in enumerate(messages):
        near = message.shape[0] == plan.near
        source = source % 2
        rows = message[pl.ds(plan.size(near), plan.extra), :].astype(jnp.float32)
        names = rows[plan.slots * plan.tap_rows : plan.slots * plan.tap_rows + 1, :]
        for slot in range(plan.slots):
            pieces = [
                rows[slot * plan.tap_rows + part : slot * plan.tap_rows + part + 1, :]
                for part in range(plan.tap_rows)
            ]
            pieces += [jnp.zeros((1, LANES), jnp.float32)] * (lanes // LANES - plan.tap_rows)
            moved = pltpu.roll(jnp.concatenate(pieces, axis=1), shift, 1)
            spread = jnp.broadcast_to(moved, (BLOCK, lanes))
            rolled = pltpu.roll(spread, 0, 1, stride=1, stride_axis=0)
            table[source, pl.ds(slot * BLOCK, BLOCK), :] = rolled[:, : plan.depth].astype(jnp.bfloat16)
        right = jnp.concatenate(
            [
                message[pl.ds(start if near else pl.multiple_of(offset + start, TILE), plan.depth), :]
                for start in plan.block_starts
            ],
            axis=1,
        )
        products = jnp.dot(table[source], right, preferred_element_type=jnp.float32)
        for slot in range(plan.slots):
            product = products[slot * BLOCK : (slot + 1) * BLOCK]
            station = names[0, slot].astype(jnp.int32)
            done = 0
            for i, start in enumerate(plan.block_starts):
                skip = done - start
                field[station, pl.ds(done, BLOCK - skip), :] += product[
                    skip:, i * LANES : (i + 1) * LANES
                ]
                done = start + BLOCK


def split_and_gram(plan, field, split_ref, gram_ref, total):
    total[...] = jnp.zeros_like(total)
    inside = lax.broadcasted_iota(jnp.int32, (plan.rows, LANES), 0) < plan.segment

    for station in range(plan.band):
        values = jnp.where(inside, field[station], 0.0)
        high = values.astype(jnp.bfloat16)
        low = (values - high.astype(jnp.float32)).astype(jnp.bfloat16)
        both = jnp.concatenate([high, low], axis=1)
        split_ref[station] = both
        total[...] += lax.dot_general(
            both, both, (((0,), (0,)), ((), ())), preferred_element_type=jnp.float32
        )

    rows = total[pl.ds(0, LANES), :] + total[pl.ds(LANES, LANES), :]
    gram_ref[...] = folded(rows[:, :LANES] + rows[:, LANES:])


def field_kernel(plan, first, last, count, band_ref, *rest):
    messages, rest = rest[:count], rest[count:]
    if not first:
        field, rest = rest[0], rest[1:]
    base = band_ref[0] * plan.segment + plan.left - plan.half
    chip = band_ref[0] // 2 * (2 * plan.segment) + plan.left - plan.half
    aligned = base // TILE * TILE
    place = (aligned - chip // TILE * TILE, base - aligned)
    if last:
        split_ref, gram_ref, table, total = rest
        add_products(plan, place, messages, field, table)
        split_and_gram(plan, field, split_ref, gram_ref, total)
    else:
        out_ref, table = rest
        if first:
            out_ref[...] = jnp.zeros_like(out_ref)
        add_products(plan, place, messages, out_ref, table)


def add_rows(plan, band, messages, field, last):
    count, first = len(messages), field is None
    vmem = pl.BlockSpec(memory_space=pltpu.VMEM)
    field_shape = jax.ShapeDtypeStruct((plan.band, plan.rows, LANES), jnp.float32)
    if last:
        out_shape = [
            jax.ShapeDtypeStruct((plan.band, plan.rows, 2 * LANES), jnp.bfloat16),
            jax.ShapeDtypeStruct((LANES * 5 // 8, LANES), jnp.float32),
        ]
    else:
        out_shape = field_shape
    operands = [band, *messages] + ([] if first else [field])
    return pl.pallas_call(
        functools.partial(field_kernel, plan, first, last, count),
        out_shape=out_shape,
        in_specs=[pl.BlockSpec(memory_space=pltpu.SMEM)] + [vmem] * (len(operands) - 1),
        out_specs=[vmem] * 2 if last else vmem,
        input_output_aliases={} if first or last else {len(operands) - 1: 0},
        scratch_shapes=[pltpu.VMEM((min(count, 2), plan.slots * BLOCK, plan.depth), jnp.bfloat16)]
        + ([pltpu.VMEM((2 * LANES, 2 * LANES), jnp.float32)] if last else []),
        compiler_params=pltpu.CompilerParams(vmem_limit_bytes=24 << 20),
        cost_estimate=pl.CostEstimate(flops=1 << 20, bytes_accessed=1 << 16, transcendentals=0),
        name="field_and_gram" if last else "field",
    )(*operands)


def three_parts(value):
    first = value.astype(jnp.bfloat16)
    value = value - first.astype(jnp.float32)
    second = value.astype(jnp.bfloat16)
    return first, second, (value - second.astype(jnp.float32)).astype(jnp.bfloat16)


def invert_factor(gram, left, right):
    size = gram.shape[0]
    row = lax.broadcasted_iota(jnp.int32, (size, size), 0)
    col = lax.broadcasted_iota(jnp.int32, (size, size), 1)
    left[...] = gram
    right[...] = (row == col).astype(jnp.float32)
    sub = lax.broadcasted_iota(jnp.int32, (8, size), 0)
    for base in range(0, size, PANEL):
        x, y = left[pl.ds(base, PANEL), :], right[pl.ds(base, PANEL), :]
        square = {}
        for i in range(PANEL):
            for k in range(i, PANEL):
                square[i, k] = jnp.broadcast_to(x[i : i + 1, base + k : base + k + 1], (8, size))
        xs = [jnp.broadcast_to(x[i : i + 1, :], (8, size)) for i in range(PANEL)]
        ys = [jnp.broadcast_to(y[i : i + 1, :], (8, size)) for i in range(PANEL)]
        for i in range(PANEL):
            scale = lax.rsqrt(square[i, i])
            scaled = {k: square[i, k] * scale for k in range(i + 1, PANEL)}
            xs[i], ys[i] = xs[i] * scale, ys[i] * scale
            for k in range(i + 1, PANEL):
                for m in range(k, PANEL):
                    square[k, m] = square[k, m] - scaled[k] * scaled[m]
                xs[k] = xs[k] - scaled[k] * xs[i]
                ys[k] = ys[k] - scaled[k] * ys[i]
        upper, lower = [], []
        for tile in range(0, PANEL, 8):
            u, v = xs[tile], ys[tile]
            for i in range(1, 8):
                u = jnp.where(sub == i, xs[tile + i], u)
                v = jnp.where(sub == i, ys[tile + i], v)
            upper.append(u)
            lower.append(v)
        u, v = jnp.concatenate(upper, axis=0), jnp.concatenate(lower, axis=0)
        right[pl.ds(base, PANEL), :] = v
        rest = size - base - PANEL
        if rest:
            a, b, c = three_parts(jnp.concatenate([u, v], axis=1))
            one = jnp.concatenate([part[:, :size] for part in (a, a, b, a, b, c)], axis=0)
            two = jnp.concatenate([a, b, a, c, b, a], axis=0)
            update = lax.dot_general(
                one, two, (((0,), (0,)), ((), ())), preferred_element_type=jnp.float32
            )[base + PANEL :]
            left[pl.ds(base + PANEL, rest), :] -= update[:, :size]
            right[pl.ds(base + PANEL, rest), :] -= update[:, size:]


def folded(gram):
    lane = lax.broadcasted_iota(jnp.int32, (32, LANES), 1)
    second = jnp.where(lane < 32, pltpu.roll(gram[96:], 32, 1), gram[32:64])
    third = jnp.where(lane[:16] < 64, pltpu.roll(gram[64:80], 64, 1), gram[80:96])
    return jnp.concatenate([gram[:32], second, third], axis=0)


def unfolded(packed):
    third = packed[64:]
    corner = pltpu.roll(packed[32:64], 96, 1)
    return jnp.concatenate([packed[:64], pltpu.roll(third, 64, 1), third, corner], axis=0)


def basis_kernel(plan, scale, addends, *rest):
    packed = rest[0][...]
    for other in rest[1:addends]:
        packed = packed + other[...]
    split_ref, out_hbm, left, right, held, sems = rest[addends:]
    invert_factor(unfolded(packed), left, right)
    weight = right[...] * scale
    high = weight.astype(jnp.bfloat16)
    low = (weight - high.astype(jnp.float32)).astype(jnp.bfloat16)
    turned = jnp.concatenate(
        [jnp.concatenate([high, high], axis=1), jnp.concatenate([low, low], axis=1)], axis=0
    )
    copies = []
    for start in range(0, plan.rows, CHUNK):
        size = min(CHUNK, plan.rows - start)
        kept = min(size, plan.segment - start)
        for station in range(plan.band):
            product = lax.dot_general(
                split_ref[station, pl.ds(start, size), :],
                turned,
                (((1,), (1,)), ((), ())),
                preferred_element_type=jnp.float32,
            )
            total = product[:, :LANES] + product[:, LANES:]
            held[pl.ds(start * plan.band + station, kept, stride=plan.band), :] = total[:kept]
        rows = pl.ds(start * plan.band, kept * plan.band)
        copies.append(pltpu.make_async_copy(held.at[rows], out_hbm.at[rows], sems.at[len(copies)]))
        copies[-1].start()
    for copy in copies:
        copy.wait()


def make_basis(plan, scale, grams, split):
    vmem = pl.BlockSpec(memory_space=pltpu.VMEM)
    shape = (plan.segment * plan.band, LANES)
    rows = pl.pallas_call(
        functools.partial(basis_kernel, plan, scale, len(grams)),
        out_shape=jax.ShapeDtypeStruct(shape, jnp.float32),
        in_specs=[vmem] * (len(grams) + 1),
        out_specs=pl.BlockSpec(memory_space=pl.ANY),
        scratch_shapes=[pltpu.VMEM((LANES, LANES), jnp.float32)] * 2
        + [pltpu.VMEM(shape, jnp.float32), pltpu.SemaphoreType.DMA((-(-plan.rows // CHUNK),))],
        compiler_params=pltpu.CompilerParams(vmem_limit_bytes=24 << 20),
        name="factor_and_basis",
    )(*grams, split)
    return rows.reshape(plan.segment, plan.band, LANES).transpose(1, 0, 2)


def sum_four(value, axis, bit):
    return value + sum(swapped(value, axis, k << bit) for k in (1, 2, 3))


def sum_over(value, axis, bits):
    while bits:
        if axis == "grp" and len(bits) > 1:
            value = sum_four(value, axis, bits[0])
            bits = bits[2:]
        else:
            value = value + swapped(value, axis, 1 << bits[0])
            bits = bits[1:]
    return value


def both_cores(values):
    return values + [swapped(value, "band", 1) for value in values]


def local(probes, kernel, pair_station, pair_count):
    length, probe_count = probes.shape[2:]
    slots, taps = kernel.shape[1], kernel.shape[3]
    band_size, grp_size = lax.axis_size("band"), lax.axis_size("grp")
    plan = Plan(length, taps, slots, band_size)
    band = lax.axis_index("band").astype(jnp.int32).reshape(1)
    messages = pack(
        plan, band, probes.reshape(length, probe_count), kernel.reshape(slots, taps), pair_station, pair_count
    )
    arrived = [
        value if mask == 0 else swapped(value, "band", mask)
        for value, (mask, near) in zip(messages, plan.sends)
    ]
    near = sum(near for _, near in plan.sends)
    field = add_rows(plan, band, both_cores(arrived[:1]), None, False)
    field = add_rows(plan, band, arrived[1 : 1 + near], field, False)
    rest, field = lax.optimization_barrier((arrived[1 + near :], field))
    passed = [swapped(value, "band", 1) for value in rest]
    field = add_rows(plan, band, rest, field, False)
    field = add_rows(plan, band, passed, field, True)
    split, gram = field
    band_bits, grp_bits = (list(range(n.bit_length() - 1)) for n in (band_size, grp_size))
    gram = sum_over(gram, "band", band_bits[:1])
    gram = sum_over(gram, "grp", grp_bits)
    gram = sum_over(gram, "band", band_bits[1:-1])
    grams = [gram, swapped(gram, "band", 1 << band_bits[-1])]
    scale = float(grp_size * band_size * length) ** 0.5
    return make_basis(plan, scale, grams, split)


def solution(mesh):
    placed = (
        P(("grp", "band"), None, None, None),
        P(("grp", "band"), None, None, None),
        P(("grp", "band"), None),
        P(("grp", "band")),
    )
    return jax.shard_map(
        local, mesh=mesh, in_specs=placed, out_specs=P("grp", "band", None), check_vma=False
    )
```

```python
import functools

import jax
import jax.numpy as jnp
from jax import lax
from jax.experimental import pallas as pl
from jax.experimental.pallas import tpu as pltpu
from jax.sharding import PartitionSpec as P

LANES = 128
TILE = 16
BLOCK = 32
PANEL = 16
CHUNK = 192


def up(value, step):
    return -(-value // step) * step


def swapped(value, axis, mask):
    pairs = [(source, source ^ mask) for source in range(lax.axis_size(axis))]
    return lax.ppermute(value, axis, pairs)


class Plan:
    def __init__(self, length, taps, slots, band_size):
        self.length, self.taps, self.slots, self.band = length, taps, slots, band_size
        self.half = (taps - 1) // 2
        self.segment = length // band_size
        starts = [b * self.segment - self.half for b in range(band_size)]
        self.aligned = [s // TILE * TILE for s in starts]
        self.shifts = [s - a for s, a in zip(starts, self.aligned)]
        self.rows = up(self.segment, TILE)
        blocks = -(-self.segment // BLOCK)
        self.block_starts = [min(i * BLOCK, self.rows - BLOCK) for i in range(blocks)]
        self.depth = up(BLOCK + taps - 1 + max(self.shifts), TILE)
        self.sub = self.block_starts[-1] + self.depth
        self.chip_starts = [self.aligned[b // 2 * 2] for b in range(band_size)]
        self.offsets = [a - c for a, c in zip(self.aligned, self.chip_starts)]
        reach = self.segment + taps - 1
        self.window = up(max(o + s + reach for o, s in zip(self.offsets, self.shifts)), TILE)
        self.left = -min(self.chip_starts)
        self.tap_rows = -(-taps // LANES)
        self.extra = up(slots * self.tap_rows + 1, TILE)
        self.whole = self.window + self.extra
        assert max(self.offsets) + self.sub <= self.whole
        self.near = self.sub + self.extra
        self.sends = [(0, False)] + [(m, True) for m in (2, 3)][: band_size - 2]
        self.sends += [(m, False) for m in range(4, band_size, 2)]

    def size(self, near):
        return self.sub if near else self.window

    def shapes(self):
        return [jax.ShapeDtypeStruct((self.size(near) + self.extra, LANES), jnp.bfloat16) for _, near in self.sends]


def pack_kernel(plan, band_ref, count_ref, station_hbm, taps_hbm, probes_hbm, *rest):
    peers = len(plan.sends)
    messages = rest[:peers]
    station_ref, taps_ref, rows_f32, in_sems, out_sems = rest[peers:]
    loads = [(station_hbm, station_ref), (taps_hbm, taps_ref)]
    loads = [pltpu.make_async_copy(a, b, in_sems.at[i]) for i, (a, b) in enumerate(loads)]
    for copy in loads:
        copy.start()

    def windows(peer, act):
        mask, near = plan.sends[peer]
        size = plan.size(near)
        other = band_ref[0] ^ mask
        if not near:
            other = other // 2 * 2
        plain = other >= 0
        for index in range(0, plan.band, 1 if near else 2):
            start = plan.aligned[index]
            if start < 0:
                first, cut = plan.length + start, -start
            elif start + size > plan.length:
                first, cut = start, plan.length - start
            else:
                continue
            plain = jnp.logical_and(plain, other != index)

            @pl.when(other == index)
            def _():
                for piece, (low, to, count) in enumerate([(first, 0, cut), (0, cut, size - cut)]):
                    act(
                        pltpu.make_async_copy(
                            probes_hbm.at[pl.ds(low, count)],
                            messages[peer].at[pl.ds(to, count)],
                            out_sems.at[2 * peer + piece],
                        )
                    )

        @pl.when(plain)
        def _():
            low = (other * plan.segment + plan.left - plan.half) // TILE * TILE - plan.left
            act(
                pltpu.make_async_copy(
                    probes_hbm.at[pl.ds(pl.multiple_of(low, TILE), size)],
                    messages[peer].at[pl.ds(0, size)],
                    out_sems.at[2 * peer],
                )
            )

    order = list(range(peers))[::-1]
    for peer in order:
        windows(peer, lambda copy: copy.start())
    rows_f32[...] = jnp.zeros_like(rows_f32)
    for copy in loads:
        copy.wait()
    live = count_ref[0]
    for slot in range(plan.slots):
        keep = (slot < live).astype(jnp.float32)
        for part in range(plan.tap_rows):
            low = part * LANES
            width = min(LANES, plan.taps - low)
            piece = taps_ref[pl.ds(slot, 1), pl.ds(low, width)].astype(jnp.float32)
            rows_f32[pl.ds(slot * plan.tap_rows + part, 1), pl.ds(0, width)] = piece * keep
    lane = lax.broadcasted_iota(jnp.int32, (1, LANES), 1)
    names = jnp.zeros((1, LANES), jnp.float32)
    for slot in range(plan.slots):
        names = jnp.where(lane == slot, station_ref[0, slot].astype(jnp.float32), names)
    rows_f32[pl.ds(plan.slots * plan.tap_rows, 1), :] = names
    rows_bf = rows_f32[...].astype(jnp.bfloat16)
    for peer in order:
        messages[peer][pl.ds(plan.size(plan.sends[peer][1]), plan.extra), :] = rows_bf
    for peer in order:
        windows(peer, lambda copy: copy.wait())


def stay(value):
    return pltpu.with_memory_space_constraint(value, pltpu.HBM)


def pack(plan, band, probes, taps, station, count):
    peers = len(plan.sends)
    hbm = pl.BlockSpec(memory_space=pltpu.HBM)
    smem = pl.BlockSpec(memory_space=pltpu.SMEM)
    return pl.pallas_call(
        functools.partial(pack_kernel, plan),
        out_shape=plan.shapes(),
        in_specs=[smem] * 2 + [hbm] * 3,
        out_specs=[pl.BlockSpec(memory_space=pltpu.VMEM)] * peers,
        scratch_shapes=[
            pltpu.SMEM(station.shape, jnp.int32),
            pltpu.VMEM(taps.shape, jnp.bfloat16),
            pltpu.VMEM((plan.extra, LANES), jnp.float32),
            pltpu.SemaphoreType.DMA((2,)),
            pltpu.SemaphoreType.DMA((2 * peers,)),
        ],
        compiler_params=pltpu.CompilerParams(vmem_limit_bytes=8 << 20),
        cost_estimate=pl.CostEstimate(flops=0, bytes_accessed=4 << 20, transcendentals=0),
        name="pack_windows",
    )(band, count, stay(station), stay(taps), stay(probes))


def add_products(plan, place, messages, field, table):
    offset, shift = place
    lanes = up(plan.depth, LANES)
    for source, message in enumerate(messages):
        near = message.shape[0] == plan.near
        source = source % 2
        rows = message[pl.ds(plan.size(near), plan.extra), :].astype(jnp.float32)
        names = rows[plan.slots * plan.tap_rows : plan.slots * plan.tap_rows + 1, :]
        for slot in range(plan.slots):
            pieces = [
                rows[slot * plan.tap_rows + part : slot * plan.tap_rows + part + 1, :]
                for part in range(plan.tap_rows)
            ]
            pieces += [jnp.zeros((1, LANES), jnp.float32)] * (lanes // LANES - plan.tap_rows)
            moved = pltpu.roll(jnp.concatenate(pieces, axis=1), shift, 1)
            spread = jnp.broadcast_to(moved, (BLOCK, lanes))
            rolled = pltpu.roll(spread, 0, 1, stride=1, stride_axis=0)
            table[source, pl.ds(slot * BLOCK, BLOCK), :] = rolled[:, : plan.depth].astype(jnp.bfloat16)
        right = jnp.concatenate(
            [
                message[pl.ds(start if near else pl.multiple_of(offset + start, TILE), plan.depth), :]
                for start in plan.block_starts
            ],
            axis=1,
        )
        products = jnp.dot(table[source], right, preferred_element_type=jnp.float32)
        for slot in range(plan.slots):
            product = products[slot * BLOCK : (slot + 1) * BLOCK]
            station = names[0, slot].astype(jnp.int32)
            done = 0
            for i, start in enumerate(plan.block_starts):
                skip = done - start
                field[station, pl.ds(done, BLOCK - skip), :] += product[
                    skip:, i * LANES : (i + 1) * LANES
                ]
                done = start + BLOCK


def split_and_gram(plan, field, split_ref, gram_ref, total):
    total[...] = jnp.zeros_like(total)
    inside = lax.broadcasted_iota(jnp.int32, (plan.rows, LANES), 0) < plan.segment

    for station in range(plan.band):
        values = jnp.where(inside, field[station], 0.0)
        high = values.astype(jnp.bfloat16)
        low = (values - high.astype(jnp.float32)).astype(jnp.bfloat16)
        both = jnp.concatenate([high, low], axis=1)
        split_ref[station] = both
        total[...] += lax.dot_general(
            both, both, (((0,), (0,)), ((), ())), preferred_element_type=jnp.float32
        )

    rows = total[pl.ds(0, LANES), :] + total[pl.ds(LANES, LANES), :]
    gram_ref[...] = folded(rows[:, :LANES] + rows[:, LANES:])


def field_kernel(plan, first, last, count, band_ref, *rest):
    messages, rest = rest[:count], rest[count:]
    if not first:
        field, rest = rest[0], rest[1:]
    base = band_ref[0] * plan.segment + plan.left - plan.half
    chip = band_ref[0] // 2 * (2 * plan.segment) + plan.left - plan.half
    aligned = base // TILE * TILE
    place = (aligned - chip // TILE * TILE, base - aligned)
    if last:
        split_ref, gram_ref, table, total = rest
        add_products(plan, place, messages, field, table)
        split_and_gram(plan, field, split_ref, gram_ref, total)
    else:
        out_ref, table = rest
        if first:
            out_ref[...] = jnp.zeros_like(out_ref)
        add_products(plan, place, messages, out_ref, table)


def add_rows(plan, band, messages, field, last):
    count, first = len(messages), field is None
    vmem = pl.BlockSpec(memory_space=pltpu.VMEM)
    field_shape = jax.ShapeDtypeStruct((plan.band, plan.rows, LANES), jnp.float32)
    if last:
        out_shape = [
            jax.ShapeDtypeStruct((plan.band, plan.rows, 2 * LANES), jnp.bfloat16),
            jax.ShapeDtypeStruct((LANES * 5 // 8, LANES), jnp.float32),
        ]
    else:
        out_shape = field_shape
    operands = [band, *messages] + ([] if first else [field])
    return pl.pallas_call(
        functools.partial(field_kernel, plan, first, last, count),
        out_shape=out_shape,
        in_specs=[pl.BlockSpec(memory_space=pltpu.SMEM)] + [vmem] * (len(operands) - 1),
        out_specs=[vmem] * 2 if last else vmem,
        input_output_aliases={} if first or last else {len(operands) - 1: 0},
        scratch_shapes=[pltpu.VMEM((min(count, 2), plan.slots * BLOCK, plan.depth), jnp.bfloat16)]
        + ([pltpu.VMEM((2 * LANES, 2 * LANES), jnp.float32)] if last else []),
        compiler_params=pltpu.CompilerParams(vmem_limit_bytes=24 << 20),
        cost_estimate=pl.CostEstimate(flops=1 << 20, bytes_accessed=1 << 16, transcendentals=0),
        name="field_and_gram" if last else "field",
    )(*operands)


def three_parts(value):
    first = value.astype(jnp.bfloat16)
    value = value - first.astype(jnp.float32)
    second = value.astype(jnp.bfloat16)
    return first, second, (value - second.astype(jnp.float32)).astype(jnp.bfloat16)


def invert_factor(gram, left, right):
    size = gram.shape[0]
    row = lax.broadcasted_iota(jnp.int32, (size, size), 0)
    col = lax.broadcasted_iota(jnp.int32, (size, size), 1)
    left[...] = gram
    right[...] = (row == col).astype(jnp.float32)
    sub = lax.broadcasted_iota(jnp.int32, (8, size), 0)
    for base in range(0, size, PANEL):
        x, y = left[pl.ds(base, PANEL), :], right[pl.ds(base, PANEL), :]
        square = {}
        for i in range(PANEL):
            for k in range(i, PANEL):
                square[i, k] = jnp.broadcast_to(x[i : i + 1, base + k : base + k + 1], (8, size))
        xs = [jnp.broadcast_to(x[i : i + 1, :], (8, size)) for i in range(PANEL)]
        ys = [jnp.broadcast_to(y[i : i + 1, :], (8, size)) for i in range(PANEL)]
        for i in range(PANEL):
            scale = lax.rsqrt(square[i, i])
            scaled = {k: square[i, k] * scale for k in range(i + 1, PANEL)}
            xs[i], ys[i] = xs[i] * scale, ys[i] * scale
            for k in range(i + 1, PANEL):
                for m in range(k, PANEL):
                    square[k, m] = square[k, m] - scaled[k] * scaled[m]
                xs[k] = xs[k] - scaled[k] * xs[i]
                ys[k] = ys[k] - scaled[k] * ys[i]
        upper, lower = [], []
        for tile in range(0, PANEL, 8):
            u, v = xs[tile], ys[tile]
            for i in range(1, 8):
                u = jnp.where(sub == i, xs[tile + i], u)
                v = jnp.where(sub == i, ys[tile + i], v)
            upper.append(u)
            lower.append(v)
        u, v = jnp.concatenate(upper, axis=0), jnp.concatenate(lower, axis=0)
        right[pl.ds(base, PANEL), :] = v
        rest = size - base - PANEL
        if rest:
            a, b, c = three_parts(jnp.concatenate([u, v], axis=1))
            one = jnp.concatenate([part[:, :size] for part in (a, a, b, a, b, c)], axis=0)
            two = jnp.concatenate([a, b, a, c, b, a], axis=0)
            update = lax.dot_general(
                one, two, (((0,), (0,)), ((), ())), preferred_element_type=jnp.float32
            )[base + PANEL :]
            left[pl.ds(base + PANEL, rest), :] -= update[:, :size]
            right[pl.ds(base + PANEL, rest), :] -= update[:, size:]


def folded(gram):
    lane = lax.broadcasted_iota(jnp.int32, (32, LANES), 1)
    second = jnp.where(lane < 32, pltpu.roll(gram[96:], 32, 1), gram[32:64])
    third = jnp.where(lane[:16] < 64, pltpu.roll(gram[64:80], 64, 1), gram[80:96])
    return jnp.concatenate([gram[:32], second, third], axis=0)


def unfolded(packed):
    third = packed[64:]
    corner = pltpu.roll(packed[32:64], 96, 1)
    return jnp.concatenate([packed[:64], pltpu.roll(third, 64, 1), third, corner], axis=0)


def basis_kernel(plan, scale, addends, *rest):
    packed = rest[0][...]
    for other in rest[1:addends]:
        packed = packed + other[...]
    split_ref, out_hbm, left, right, held, sems = rest[addends:]
    invert_factor(unfolded(packed), left, right)
    weight = right[...] * scale
    high = weight.astype(jnp.bfloat16)
    low = (weight - high.astype(jnp.float32)).astype(jnp.bfloat16)
    turned = jnp.concatenate(
        [jnp.concatenate([high, high], axis=1), jnp.concatenate([low, low], axis=1)], axis=0
    )
    copies = []
    for start in range(0, plan.rows, CHUNK):
        size = min(CHUNK, plan.rows - start)
        kept = min(size, plan.segment - start)
        for station in range(plan.band):
            product = lax.dot_general(
                split_ref[station, pl.ds(start, size), :],
                turned,
                (((1,), (1,)), ((), ())),
                preferred_element_type=jnp.float32,
            )
            total = product[:, :LANES] + product[:, LANES:]
            held[pl.ds(start * plan.band + station, size, stride=plan.band), :] = total
        rows = pl.ds(start * plan.band, kept * plan.band)
        copies.append(pltpu.make_async_copy(held.at[rows], out_hbm.at[rows], sems.at[len(copies)]))
        copies[-1].start()
    for copy in copies:
        copy.wait()


def make_basis(plan, scale, grams, split):
    vmem = pl.BlockSpec(memory_space=pltpu.VMEM)
    shape = (plan.segment * plan.band, LANES)
    rows = pl.pallas_call(
        functools.partial(basis_kernel, plan, scale, len(grams)),
        out_shape=jax.ShapeDtypeStruct(shape, jnp.float32),
        in_specs=[vmem] * (len(grams) + 1),
        out_specs=pl.BlockSpec(memory_space=pl.ANY),
        scratch_shapes=[pltpu.VMEM((LANES, LANES), jnp.float32)] * 2
        + [pltpu.VMEM((plan.rows * plan.band, LANES), jnp.float32), pltpu.SemaphoreType.DMA((-(-plan.rows // CHUNK),))],
        compiler_params=pltpu.CompilerParams(vmem_limit_bytes=24 << 20),
        name="factor_and_basis",
    )(*grams, split)
    return rows.reshape(plan.segment, plan.band, LANES).transpose(1, 0, 2)


def sum_four(value, axis, bit):
    return value + sum(swapped(value, axis, k << bit) for k in (1, 2, 3))


def sum_over(value, axis, bits):
    while bits:
        if axis == "grp" and len(bits) > 1:
            value = sum_four(value, axis, bits[0])
            bits = bits[2:]
        else:
            value = value + swapped(value, axis, 1 << bits[0])
            bits = bits[1:]
    return value


def both_cores(values):
    return values + [swapped(value, "band", 1) for value in values]


def local(probes, kernel, pair_station, pair_count):
    length, probe_count = probes.shape[2:]
    slots, taps = kernel.shape[1], kernel.shape[3]
    band_size, grp_size = lax.axis_size("band"), lax.axis_size("grp")
    plan = Plan(length, taps, slots, band_size)
    band = lax.axis_index("band").astype(jnp.int32).reshape(1)
    messages = pack(
        plan, band, probes.reshape(length, probe_count), kernel.reshape(slots, taps), pair_station, pair_count
    )
    arrived = [
        value if mask == 0 else swapped(value, "band", mask)
        for value, (mask, near) in zip(messages, plan.sends)
    ]
    near = sum(near for _, near in plan.sends)
    field = add_rows(plan, band, both_cores(arrived[:1]), None, False)
    field = add_rows(plan, band, arrived[1 : 1 + near], field, False)
    *head, tail = arrived[1 + near :]
    passed = [swapped(value, "band", 1) for value in head]
    field = add_rows(plan, band, head, field, False)
    tail, field = lax.optimization_barrier((tail, field))
    tail_passed = swapped(tail, "band", 1)
    field = add_rows(plan, band, [tail, *passed], field, False)
    field = add_rows(plan, band, [tail_passed], field, True)
    split, gram = field
    band_bits, grp_bits = (list(range(n.bit_length() - 1)) for n in (band_size, grp_size))
    gram = sum_over(gram, "band", band_bits[:1])
    gram = sum_over(gram, "grp", grp_bits)
    gram = sum_over(gram, "band", band_bits[1:-1])
    grams = [gram, swapped(gram, "band", 1 << band_bits[-1])]
    scale = float(grp_size * band_size * length) ** 0.5
    return make_basis(plan, scale, grams, split)


def solution(mesh):
    placed = (
        P(("grp", "band"), None, None, None),
        P(("grp", "band"), None, None, None),
        P(("grp", "band"), None),
        P(("grp", "band")),
    )
    return jax.shard_map(
        local, mesh=mesh, in_specs=placed, out_specs=P("grp", "band", None), check_vma=False
    )
```

```python
import functools

import jax
import jax.numpy as jnp
from jax import lax
from jax.experimental import pallas as pl
from jax.experimental.pallas import tpu as pltpu
from jax.sharding import PartitionSpec as P

LANES = 128
TILE = 16
BLOCK = 32
PANEL = 16
CHUNK = 272


def up(value, step):
    return -(-value // step) * step


def swapped(value, axis, mask):
    pairs = [(source, source ^ mask) for source in range(lax.axis_size(axis))]
    return lax.ppermute(value, axis, pairs)


class Plan:
    def __init__(self, length, taps, slots, band_size):
        self.length, self.taps, self.slots, self.band = length, taps, slots, band_size
        self.half = (taps - 1) // 2
        self.segment = length // band_size
        starts = [b * self.segment - self.half for b in range(band_size)]
        self.aligned = [s // TILE * TILE for s in starts]
        self.shifts = [s - a for s, a in zip(starts, self.aligned)]
        self.rows = up(self.segment, TILE)
        blocks = -(-self.segment // BLOCK)
        self.block_starts = [min(i * BLOCK, self.rows - BLOCK) for i in range(blocks)]
        self.depth = up(BLOCK + taps - 1 + max(self.shifts), TILE)
        self.sub = self.block_starts[-1] + self.depth
        self.chip_starts = [self.aligned[b // 2 * 2] for b in range(band_size)]
        self.offsets = [a - c for a, c in zip(self.aligned, self.chip_starts)]
        reach = self.segment + taps - 1
        self.window = up(max(o + s + reach for o, s in zip(self.offsets, self.shifts)), TILE)
        self.left = -min(self.chip_starts)
        self.tap_rows = -(-taps // LANES)
        self.extra = up(slots * self.tap_rows + 1, TILE)
        self.whole = self.window + self.extra
        assert max(self.offsets) + self.sub <= self.whole
        self.near = self.sub + self.extra
        self.sends = [(0, False)] + [(m, True) for m in (2, 3)][: band_size - 2]
        self.sends += [(m, False) for m in range(4, band_size, 2)]

    def size(self, near):
        return self.sub if near else self.window

    def shapes(self):
        return [jax.ShapeDtypeStruct((self.size(near) + self.extra, LANES), jnp.bfloat16) for _, near in self.sends]


def pack_kernel(plan, band_ref, count_ref, station_hbm, taps_hbm, probes_hbm, *rest):
    peers = len(plan.sends)
    messages = rest[:peers]
    station_ref, taps_ref, rows_f32, in_sems, out_sems = rest[peers:]
    loads = [(station_hbm, station_ref), (taps_hbm, taps_ref)]
    loads = [pltpu.make_async_copy(a, b, in_sems.at[i]) for i, (a, b) in enumerate(loads)]
    for copy in loads:
        copy.start()

    def windows(peer, act):
        mask, near = plan.sends[peer]
        size = plan.size(near)
        other = band_ref[0] ^ mask
        if not near:
            other = other // 2 * 2
        plain = other >= 0
        for index in range(0, plan.band, 1 if near else 2):
            start = plan.aligned[index]
            if start < 0:
                first, cut = plan.length + start, -start
            elif start + size > plan.length:
                first, cut = start, plan.length - start
            else:
                continue
            plain = jnp.logical_and(plain, other != index)

            @pl.when(other == index)
            def _():
                for piece, (low, to, count) in enumerate([(first, 0, cut), (0, cut, size - cut)]):
                    act(
                        pltpu.make_async_copy(
                            probes_hbm.at[pl.ds(low, count)],
                            messages[peer].at[pl.ds(to, count)],
                            out_sems.at[2 * peer + piece],
                        )
                    )

        @pl.when(plain)
        def _():
            low = (other * plan.segment + plan.left - plan.half) // TILE * TILE - plan.left
            act(
                pltpu.make_async_copy(
                    probes_hbm.at[pl.ds(pl.multiple_of(low, TILE), size)],
                    messages[peer].at[pl.ds(0, size)],
                    out_sems.at[2 * peer],
                )
            )

    order = list(range(peers))[::-1]
    for peer in order:
        windows(peer, lambda copy: copy.start())
    rows_f32[...] = jnp.zeros_like(rows_f32)
    for copy in loads:
        copy.wait()
    live = count_ref[0]
    for slot in range(plan.slots):
        keep = (slot < live).astype(jnp.float32)
        for part in range(plan.tap_rows):
            low = part * LANES
            width = min(LANES, plan.taps - low)
            piece = taps_ref[pl.ds(slot, 1), pl.ds(low, width)].astype(jnp.float32)
            rows_f32[pl.ds(slot * plan.tap_rows + part, 1), pl.ds(0, width)] = piece * keep
    lane = lax.broadcasted_iota(jnp.int32, (1, LANES), 1)
    names = jnp.zeros((1, LANES), jnp.float32)
    for slot in range(plan.slots):
        names = jnp.where(lane == slot, station_ref[0, slot].astype(jnp.float32), names)
    rows_f32[pl.ds(plan.slots * plan.tap_rows, 1), :] = names
    rows_bf = rows_f32[...].astype(jnp.bfloat16)
    for peer in order:
        messages[peer][pl.ds(plan.size(plan.sends[peer][1]), plan.extra), :] = rows_bf
    for peer in order:
        windows(peer, lambda copy: copy.wait())


def stay(value):
    return pltpu.with_memory_space_constraint(value, pltpu.HBM)


def pack(plan, band, probes, taps, station, count):
    peers = len(plan.sends)
    hbm = pl.BlockSpec(memory_space=pltpu.HBM)
    smem = pl.BlockSpec(memory_space=pltpu.SMEM)
    return pl.pallas_call(
        functools.partial(pack_kernel, plan),
        out_shape=plan.shapes(),
        in_specs=[smem] * 2 + [hbm] * 3,
        out_specs=[pl.BlockSpec(memory_space=pltpu.VMEM)] * peers,
        scratch_shapes=[
            pltpu.SMEM(station.shape, jnp.int32),
            pltpu.VMEM(taps.shape, jnp.bfloat16),
            pltpu.VMEM((plan.extra, LANES), jnp.float32),
            pltpu.SemaphoreType.DMA((2,)),
            pltpu.SemaphoreType.DMA((2 * peers,)),
        ],
        compiler_params=pltpu.CompilerParams(vmem_limit_bytes=8 << 20),
        cost_estimate=pl.CostEstimate(flops=0, bytes_accessed=4 << 20, transcendentals=0),
        name="pack_windows",
    )(band, count, stay(station), stay(taps), stay(probes))


def add_products(plan, place, messages, field, table):
    offset, shift = place
    lanes = up(plan.depth, LANES)
    for source, message in enumerate(messages):
        near = message.shape[0] == plan.near
        source = source % 2
        rows = message[pl.ds(plan.size(near), plan.extra), :].astype(jnp.float32)
        names = rows[plan.slots * plan.tap_rows : plan.slots * plan.tap_rows + 1, :]
        for slot in range(plan.slots):
            pieces = [
                rows[slot * plan.tap_rows + part : slot * plan.tap_rows + part + 1, :]
                for part in range(plan.tap_rows)
            ]
            pieces += [jnp.zeros((1, LANES), jnp.float32)] * (lanes // LANES - plan.tap_rows)
            moved = pltpu.roll(jnp.concatenate(pieces, axis=1), shift, 1)
            spread = jnp.broadcast_to(moved, (BLOCK, lanes))
            rolled = pltpu.roll(spread, 0, 1, stride=1, stride_axis=0)
            table[source, pl.ds(slot * BLOCK, BLOCK), :] = rolled[:, : plan.depth].astype(jnp.bfloat16)
        right = jnp.concatenate(
            [
                message[pl.ds(start if near else pl.multiple_of(offset + start, TILE), plan.depth), :]
                for start in plan.block_starts
            ],
            axis=1,
        )
        products = jnp.dot(table[source], right, preferred_element_type=jnp.float32)
        for slot in range(plan.slots):
            product = products[slot * BLOCK : (slot + 1) * BLOCK]
            station = names[0, slot].astype(jnp.int32)
            done = 0
            for i, start in enumerate(plan.block_starts):
                skip = done - start
                field[station, pl.ds(done, BLOCK - skip), :] += product[
                    skip:, i * LANES : (i + 1) * LANES
                ]
                done = start + BLOCK


def split_and_gram(plan, field, split_ref, gram_ref, total):
    total[...] = jnp.zeros_like(total)
    inside = lax.broadcasted_iota(jnp.int32, (plan.rows, LANES), 0) < plan.segment

    for station in range(plan.band):
        values = jnp.where(inside, field[station], 0.0)
        high = values.astype(jnp.bfloat16)
        low = (values - high.astype(jnp.float32)).astype(jnp.bfloat16)
        both = jnp.concatenate([high, low], axis=1)
        split_ref[station] = both
        total[...] += lax.dot_general(
            both, both, (((0,), (0,)), ((), ())), preferred_element_type=jnp.float32
        )

    rows = total[pl.ds(0, LANES), :] + total[pl.ds(LANES, LANES), :]
    gram_ref[...] = folded(rows[:, :LANES] + rows[:, LANES:])


def field_kernel(plan, first, last, count, band_ref, *rest):
    messages, rest = rest[:count], rest[count:]
    if not first:
        field, rest = rest[0], rest[1:]
    base = band_ref[0] * plan.segment + plan.left - plan.half
    chip = band_ref[0] // 2 * (2 * plan.segment) + plan.left - plan.half
    aligned = base // TILE * TILE
    place = (aligned - chip // TILE * TILE, base - aligned)
    if last:
        split_ref, gram_ref, table, total = rest
        add_products(plan, place, messages, field, table)
        split_and_gram(plan, field, split_ref, gram_ref, total)
    else:
        out_ref, table = rest
        if first:
            out_ref[...] = jnp.zeros_like(out_ref)
        add_products(plan, place, messages, out_ref, table)


def add_rows(plan, band, messages, field, last):
    count, first = len(messages), field is None
    vmem = pl.BlockSpec(memory_space=pltpu.VMEM)
    field_shape = jax.ShapeDtypeStruct((plan.band, plan.rows, LANES), jnp.float32)
    if last:
        out_shape = [
            jax.ShapeDtypeStruct((plan.band, plan.rows, 2 * LANES), jnp.bfloat16),
            jax.ShapeDtypeStruct((LANES * 5 // 8, LANES), jnp.float32),
        ]
    else:
        out_shape = field_shape
    operands = [band, *messages] + ([] if first else [field])
    return pl.pallas_call(
        functools.partial(field_kernel, plan, first, last, count),
        out_shape=out_shape,
        in_specs=[pl.BlockSpec(memory_space=pltpu.SMEM)] + [vmem] * (len(operands) - 1),
        out_specs=[vmem] * 2 if last else vmem,
        input_output_aliases={} if first or last else {len(operands) - 1: 0},
        scratch_shapes=[pltpu.VMEM((min(count, 2), plan.slots * BLOCK, plan.depth), jnp.bfloat16)]
        + ([pltpu.VMEM((2 * LANES, 2 * LANES), jnp.float32)] if last else []),
        compiler_params=pltpu.CompilerParams(vmem_limit_bytes=24 << 20),
        cost_estimate=pl.CostEstimate(flops=1 << 20, bytes_accessed=1 << 16, transcendentals=0),
        name="field_and_gram" if last else "field",
    )(*operands)


def three_parts(value):
    first = value.astype(jnp.bfloat16)
    value = value - first.astype(jnp.float32)
    second = value.astype(jnp.bfloat16)
    return first, second, (value - second.astype(jnp.float32)).astype(jnp.bfloat16)


def invert_factor(gram, left, right):
    size = gram.shape[0]
    row = lax.broadcasted_iota(jnp.int32, (size, size), 0)
    col = lax.broadcasted_iota(jnp.int32, (size, size), 1)
    left[...] = gram
    right[...] = (row == col).astype(jnp.float32)
    sub = lax.broadcasted_iota(jnp.int32, (8, size), 0)
    for base in range(0, size, PANEL):
        x, y = left[pl.ds(base, PANEL), :], right[pl.ds(base, PANEL), :]
        square = {}
        for i in range(PANEL):
            for k in range(i, PANEL):
                square[i, k] = jnp.broadcast_to(x[i : i + 1, base + k : base + k + 1], (8, size))
        xs = [jnp.broadcast_to(x[i : i + 1, :], (8, size)) for i in range(PANEL)]
        ys = [jnp.broadcast_to(y[i : i + 1, :], (8, size)) for i in range(PANEL)]
        for i in range(PANEL):
            scale = lax.rsqrt(square[i, i])
            scaled = {k: square[i, k] * scale for k in range(i + 1, PANEL)}
            xs[i], ys[i] = xs[i] * scale, ys[i] * scale
            for k in range(i + 1, PANEL):
                for m in range(k, PANEL):
                    square[k, m] = square[k, m] - scaled[k] * scaled[m]
                xs[k] = xs[k] - scaled[k] * xs[i]
                ys[k] = ys[k] - scaled[k] * ys[i]
        upper, lower = [], []
        for tile in range(0, PANEL, 8):
            u, v = xs[tile], ys[tile]
            for i in range(1, 8):
                u = jnp.where(sub == i, xs[tile + i], u)
                v = jnp.where(sub == i, ys[tile + i], v)
            upper.append(u)
            lower.append(v)
        u, v = jnp.concatenate(upper, axis=0), jnp.concatenate(lower, axis=0)
        right[pl.ds(base, PANEL), :] = v
        rest = size - base - PANEL
        if rest:
            a, b, c = three_parts(jnp.concatenate([u, v], axis=1))
            one = jnp.concatenate([part[:, :size] for part in (a, a, b, a, b, c)], axis=0)
            two = jnp.concatenate([a, b, a, c, b, a], axis=0)
            update = lax.dot_general(
                one, two, (((0,), (0,)), ((), ())), preferred_element_type=jnp.float32
            )[base + PANEL :]
            left[pl.ds(base + PANEL, rest), :] -= update[:, :size]
            right[pl.ds(base + PANEL, rest), :] -= update[:, size:]


def folded(gram):
    lane = lax.broadcasted_iota(jnp.int32, (32, LANES), 1)
    second = jnp.where(lane < 32, pltpu.roll(gram[96:], 32, 1), gram[32:64])
    third = jnp.where(lane[:16] < 64, pltpu.roll(gram[64:80], 64, 1), gram[80:96])
    return jnp.concatenate([gram[:32], second, third], axis=0)


def unfolded(packed):
    third = packed[64:]
    corner = pltpu.roll(packed[32:64], 96, 1)
    return jnp.concatenate([packed[:64], pltpu.roll(third, 64, 1), third, corner], axis=0)


def basis_kernel(plan, scale, addends, *rest):
    packed = rest[0][...]
    for other in rest[1:addends]:
        packed = packed + other[...]
    split_ref, out_hbm, left, right, held, sems = rest[addends:]
    invert_factor(unfolded(packed), left, right)
    weight = right[...] * scale
    high = weight.astype(jnp.bfloat16)
    low = (weight - high.astype(jnp.float32)).astype(jnp.bfloat16)
    turned = jnp.concatenate(
        [jnp.concatenate([high, high], axis=1), jnp.concatenate([low, low], axis=1)], axis=0
    )
    copies = []
    for start in range(0, plan.rows, CHUNK):
        size = min(CHUNK, plan.rows - start)
        kept = min(size, plan.segment - start)
        for station in range(plan.band):
            product = lax.dot_general(
                split_ref[station, pl.ds(start, size), :],
                turned,
                (((1,), (1,)), ((), ())),
                preferred_element_type=jnp.float32,
            )
            total = product[:, :LANES] + product[:, LANES:]
            held[pl.ds(start * plan.band + station, size, stride=plan.band), :] = total
        rows = pl.ds(start * plan.band, kept * plan.band)
        copies.append(pltpu.make_async_copy(held.at[rows], out_hbm.at[rows], sems.at[len(copies)]))
        copies[-1].start()
    for copy in copies:
        copy.wait()


def make_basis(plan, scale, grams, split):
    vmem = pl.BlockSpec(memory_space=pltpu.VMEM)
    shape = (plan.segment * plan.band, LANES)
    rows = pl.pallas_call(
        functools.partial(basis_kernel, plan, scale, len(grams)),
        out_shape=jax.ShapeDtypeStruct(shape, jnp.float32),
        in_specs=[vmem] * (len(grams) + 1),
        out_specs=pl.BlockSpec(memory_space=pl.ANY),
        scratch_shapes=[pltpu.VMEM((LANES, LANES), jnp.float32)] * 2
        + [pltpu.VMEM((plan.rows * plan.band, LANES), jnp.float32), pltpu.SemaphoreType.DMA((-(-plan.rows // CHUNK),))],
        compiler_params=pltpu.CompilerParams(vmem_limit_bytes=24 << 20),
        name="factor_and_basis",
    )(*grams, split)
    return rows.reshape(plan.segment, plan.band, LANES).transpose(1, 0, 2)


def sum_four(value, axis, bit):
    return value + sum(swapped(value, axis, k << bit) for k in (1, 2, 3))


def sum_over(value, axis, bits):
    while bits:
        if len(bits) > 1:
            value = sum_four(value, axis, bits[0])
            bits = bits[2:]
        else:
            value = value + swapped(value, axis, 1 << bits[0])
            bits = bits[1:]
    return value


def both_cores(values):
    return values + [swapped(value, "band", 1) for value in values]


def local(probes, kernel, pair_station, pair_count):
    length, probe_count = probes.shape[2:]
    slots, taps = kernel.shape[1], kernel.shape[3]
    band_size, grp_size = lax.axis_size("band"), lax.axis_size("grp")
    plan = Plan(length, taps, slots, band_size)
    band = lax.axis_index("band").astype(jnp.int32).reshape(1)
    messages = pack(
        plan, band, probes.reshape(length, probe_count), kernel.reshape(slots, taps), pair_station, pair_count
    )
    arrived = [
        value if mask == 0 else swapped(value, "band", mask)
        for value, (mask, near) in zip(messages, plan.sends)
    ]
    near = sum(near for _, near in plan.sends)
    field = add_rows(plan, band, both_cores(arrived[:1]), None, False)
    field = add_rows(plan, band, arrived[1 : 1 + near], field, False)
    *head, tail = arrived[1 + near :]
    passed = [swapped(value, "band", 1) for value in head]
    field = add_rows(plan, band, head, field, False)
    tail, field = lax.optimization_barrier((tail, field))
    tail_passed = swapped(tail, "band", 1)
    field = add_rows(plan, band, [tail, *passed], field, False)
    field = add_rows(plan, band, [tail_passed], field, True)
    split, gram = field
    band_bits, grp_bits = (list(range(n.bit_length() - 1)) for n in (band_size, grp_size))
    gram = sum_over(gram, "band", band_bits[:1])
    gram = sum_over(gram, "grp", grp_bits)
    gram = sum_over(gram, "band", band_bits[1:-2])
    grams = [gram] + [swapped(gram, "band", k << band_bits[-2]) for k in (1, 2, 3)]
    scale = float(grp_size * band_size * length) ** 0.5
    return make_basis(plan, scale, grams, split)


def solution(mesh):
    placed = (
        P(("grp", "band"), None, None, None),
        P(("grp", "band"), None, None, None),
        P(("grp", "band"), None),
        P(("grp", "band")),
    )
    return jax.shard_map(
        local, mesh=mesh, in_specs=placed, out_specs=P("grp", "band", None), check_vma=False
    )
```

```python
import functools

import jax
import jax.numpy as jnp
from jax import lax
from jax.experimental import pallas as pl
from jax.experimental.pallas import tpu as pltpu
from jax.sharding import PartitionSpec as P

LANES = 128
TILE = 16
BLOCK = 32
PANEL = 16
CHUNK = 272


def up(value, step):
    return -(-value // step) * step


def swapped(value, axis, mask):
    pairs = [(source, source ^ mask) for source in range(lax.axis_size(axis))]
    return lax.ppermute(value, axis, pairs)


class Plan:
    def __init__(self, length, taps, slots, band_size):
        self.length, self.taps, self.slots, self.band = length, taps, slots, band_size
        self.half = (taps - 1) // 2
        self.segment = length // band_size
        starts = [b * self.segment - self.half for b in range(band_size)]
        self.aligned = [s // TILE * TILE for s in starts]
        self.shifts = [s - a for s, a in zip(starts, self.aligned)]
        self.rows = up(self.segment, TILE)
        blocks = -(-self.segment // BLOCK)
        self.block_starts = [min(i * BLOCK, self.rows - BLOCK) for i in range(blocks)]
        self.depth = up(BLOCK + taps - 1 + max(self.shifts), TILE)
        self.sub = self.block_starts[-1] + self.depth
        self.chip_starts = [self.aligned[b // 2 * 2] for b in range(band_size)]
        self.offsets = [a - c for a, c in zip(self.aligned, self.chip_starts)]
        reach = self.segment + taps - 1
        self.window = up(max(o + s + reach for o, s in zip(self.offsets, self.shifts)), TILE)
        self.left = -min(self.chip_starts)
        self.tap_rows = -(-taps // LANES)
        self.extra = up(slots * self.tap_rows + 1, TILE)
        self.whole = self.window + self.extra
        assert max(self.offsets) + self.sub <= self.whole
        self.near = self.sub + self.extra
        self.sends = [(0, False)] + [(m, True) for m in (2, 3)][: band_size - 2]
        self.sends += [(m, False) for m in range(4, band_size, 2)]

    def size(self, near):
        return self.sub if near else self.window

    def shapes(self):
        return [jax.ShapeDtypeStruct((self.size(near) + self.extra, LANES), jnp.bfloat16) for _, near in self.sends]


def pack_kernel(plan, band_ref, count_ref, station_hbm, taps_hbm, probes_hbm, *rest):
    peers = len(plan.sends)
    messages = rest[:peers]
    station_ref, taps_ref, rows_f32, in_sems, out_sems = rest[peers:]
    loads = [(station_hbm, station_ref), (taps_hbm, taps_ref)]
    loads = [pltpu.make_async_copy(a, b, in_sems.at[i]) for i, (a, b) in enumerate(loads)]
    for copy in loads:
        copy.start()

    def windows(peer, act):
        mask, near = plan.sends[peer]
        size = plan.size(near)
        other = band_ref[0] ^ mask
        if not near:
            other = other // 2 * 2
        plain = other >= 0
        for index in range(0, plan.band, 1 if near else 2):
            start = plan.aligned[index]
            if start < 0:
                first, cut = plan.length + start, -start
            elif start + size > plan.length:
                first, cut = start, plan.length - start
            else:
                continue
            plain = jnp.logical_and(plain, other != index)

            @pl.when(other == index)
            def _():
                for piece, (low, to, count) in enumerate([(first, 0, cut), (0, cut, size - cut)]):
                    act(
                        pltpu.make_async_copy(
                            probes_hbm.at[pl.ds(low, count)],
                            messages[peer].at[pl.ds(to, count)],
                            out_sems.at[2 * peer + piece],
                        )
                    )

        @pl.when(plain)
        def _():
            low = (other * plan.segment + plan.left - plan.half) // TILE * TILE - plan.left
            act(
                pltpu.make_async_copy(
                    probes_hbm.at[pl.ds(pl.multiple_of(low, TILE), size)],
                    messages[peer].at[pl.ds(0, size)],
                    out_sems.at[2 * peer],
                )
            )

    order = list(range(peers))[::-1]
    for peer in order:
        windows(peer, lambda copy: copy.start())
    rows_f32[...] = jnp.zeros_like(rows_f32)
    for copy in loads:
        copy.wait()
    live = count_ref[0]
    for slot in range(plan.slots):
        keep = (slot < live).astype(jnp.float32)
        for part in range(plan.tap_rows):
            low = part * LANES
            width = min(LANES, plan.taps - low)
            piece = taps_ref[pl.ds(slot, 1), pl.ds(low, width)].astype(jnp.float32)
            rows_f32[pl.ds(slot * plan.tap_rows + part, 1), pl.ds(0, width)] = piece * keep
    lane = lax.broadcasted_iota(jnp.int32, (1, LANES), 1)
    names = jnp.zeros((1, LANES), jnp.float32)
    for slot in range(plan.slots):
        names = jnp.where(lane == slot, station_ref[0, slot].astype(jnp.float32), names)
    rows_f32[pl.ds(plan.slots * plan.tap_rows, 1), :] = names
    rows_bf = rows_f32[...].astype(jnp.bfloat16)
    for peer in order:
        messages[peer][pl.ds(plan.size(plan.sends[peer][1]), plan.extra), :] = rows_bf
    for peer in order:
        windows(peer, lambda copy: copy.wait())


def stay(value):
    return pltpu.with_memory_space_constraint(value, pltpu.HBM)


def pack(plan, band, probes, taps, station, count):
    peers = len(plan.sends)
    hbm = pl.BlockSpec(memory_space=pltpu.HBM)
    smem = pl.BlockSpec(memory_space=pltpu.SMEM)
    return pl.pallas_call(
        functools.partial(pack_kernel, plan),
        out_shape=plan.shapes(),
        in_specs=[smem] * 2 + [hbm] * 3,
        out_specs=[pl.BlockSpec(memory_space=pltpu.VMEM)] * peers,
        scratch_shapes=[
            pltpu.SMEM(station.shape, jnp.int32),
            pltpu.VMEM(taps.shape, jnp.bfloat16),
            pltpu.VMEM((plan.extra, LANES), jnp.float32),
            pltpu.SemaphoreType.DMA((2,)),
            pltpu.SemaphoreType.DMA((2 * peers,)),
        ],
        compiler_params=pltpu.CompilerParams(vmem_limit_bytes=8 << 20),
        cost_estimate=pl.CostEstimate(flops=0, bytes_accessed=4 << 20, transcendentals=0),
        name="pack_windows",
    )(band, count, stay(station), stay(taps), stay(probes))


def add_products(plan, place, messages, field, table):
    offset, shift = place
    lanes = up(plan.depth, LANES)
    for source, message in enumerate(messages):
        near = message.shape[0] == plan.near
        source = source % 2
        rows = message[pl.ds(plan.size(near), plan.extra), :].astype(jnp.float32)
        names = rows[plan.slots * plan.tap_rows : plan.slots * plan.tap_rows + 1, :]
        for slot in range(plan.slots):
            pieces = [
                rows[slot * plan.tap_rows + part : slot * plan.tap_rows + part + 1, :]
                for part in range(plan.tap_rows)
            ]
            pieces += [jnp.zeros((1, LANES), jnp.float32)] * (lanes // LANES - plan.tap_rows)
            moved = pltpu.roll(jnp.concatenate(pieces, axis=1), shift, 1)
            spread = jnp.broadcast_to(moved, (BLOCK, lanes))
            rolled = pltpu.roll(spread, 0, 1, stride=1, stride_axis=0)
            table[source, pl.ds(slot * BLOCK, BLOCK), :] = rolled[:, : plan.depth].astype(jnp.bfloat16)
        right = jnp.concatenate(
            [
                message[pl.ds(start if near else pl.multiple_of(offset + start, TILE), plan.depth), :]
                for start in plan.block_starts
            ],
            axis=1,
        )
        products = jnp.dot(table[source], right, preferred_element_type=jnp.float32)
        for slot in range(plan.slots):
            product = products[slot * BLOCK : (slot + 1) * BLOCK]
            station = names[0, slot].astype(jnp.int32)
            done = 0
            for i, start in enumerate(plan.block_starts):
                skip = done - start
                field[station, pl.ds(done, BLOCK - skip), :] += product[
                    skip:, i * LANES : (i + 1) * LANES
                ]
                done = start + BLOCK


def split_and_gram(plan, field, split_ref, gram_ref, total):
    total[...] = jnp.zeros_like(total)
    inside = lax.broadcasted_iota(jnp.int32, (plan.rows, LANES), 0) < plan.segment

    for station in range(plan.band):
        values = jnp.where(inside, field[station], 0.0)
        high = values.astype(jnp.bfloat16)
        low = (values - high.astype(jnp.float32)).astype(jnp.bfloat16)
        both = jnp.concatenate([high, low], axis=1)
        split_ref[station] = both
        total[...] += lax.dot_general(
            both, both, (((0,), (0,)), ((), ())), preferred_element_type=jnp.float32
        )

    rows = total[pl.ds(0, LANES), :] + total[pl.ds(LANES, LANES), :]
    gram_ref[...] = folded(rows[:, :LANES] + rows[:, LANES:])


def field_kernel(plan, first, last, count, band_ref, *rest):
    messages, rest = rest[:count], rest[count:]
    if not first:
        field, rest = rest[0], rest[1:]
    base = band_ref[0] * plan.segment + plan.left - plan.half
    chip = band_ref[0] // 2 * (2 * plan.segment) + plan.left - plan.half
    aligned = base // TILE * TILE
    place = (aligned - chip // TILE * TILE, base - aligned)
    if last:
        split_ref, gram_ref, table, total = rest
        add_products(plan, place, messages, field, table)
        split_and_gram(plan, field, split_ref, gram_ref, total)
    else:
        out_ref, table = rest
        if first:
            out_ref[...] = jnp.zeros_like(out_ref)
        add_products(plan, place, messages, out_ref, table)


def add_rows(plan, band, messages, field, last):
    count, first = len(messages), field is None
    vmem = pl.BlockSpec(memory_space=pltpu.VMEM)
    field_shape = jax.ShapeDtypeStruct((plan.band, plan.rows, LANES), jnp.float32)
    if last:
        out_shape = [
            jax.ShapeDtypeStruct((plan.band, plan.rows, 2 * LANES), jnp.bfloat16),
            jax.ShapeDtypeStruct((LANES * 5 // 8, LANES), jnp.float32),
        ]
    else:
        out_shape = field_shape
    operands = [band, *messages] + ([] if first else [field])
    return pl.pallas_call(
        functools.partial(field_kernel, plan, first, last, count),
        out_shape=out_shape,
        in_specs=[pl.BlockSpec(memory_space=pltpu.SMEM)] + [vmem] * (len(operands) - 1),
        out_specs=[vmem] * 2 if last else vmem,
        input_output_aliases={} if first or last else {len(operands) - 1: 0},
        scratch_shapes=[pltpu.VMEM((min(count, 2), plan.slots * BLOCK, plan.depth), jnp.bfloat16)]
        + ([pltpu.VMEM((2 * LANES, 2 * LANES), jnp.float32)] if last else []),
        compiler_params=pltpu.CompilerParams(vmem_limit_bytes=24 << 20),
        cost_estimate=pl.CostEstimate(flops=1 << 20, bytes_accessed=1 << 16, transcendentals=0),
        name="field_and_gram" if last else "field",
    )(*operands)


def three_parts(value):
    first = value.astype(jnp.bfloat16)
    value = value - first.astype(jnp.float32)
    second = value.astype(jnp.bfloat16)
    return first, second, (value - second.astype(jnp.float32)).astype(jnp.bfloat16)


def invert_factor(gram, left, right):
    size = gram.shape[0]
    row = lax.broadcasted_iota(jnp.int32, (size, size), 0)
    col = lax.broadcasted_iota(jnp.int32, (size, size), 1)
    left[...] = gram
    right[...] = (row == col).astype(jnp.float32)
    sub = lax.broadcasted_iota(jnp.int32, (8, size), 0)
    for base in range(0, size, PANEL):
        x, y = left[pl.ds(base, PANEL), :], right[pl.ds(base, PANEL), :]
        square = {}
        for i in range(PANEL):
            for k in range(i, PANEL):
                square[i, k] = jnp.broadcast_to(x[i : i + 1, base + k : base + k + 1], (8, size))
        xs = [jnp.broadcast_to(x[i : i + 1, :], (8, size)) for i in range(PANEL)]
        ys = [jnp.broadcast_to(y[i : i + 1, :], (8, size)) for i in range(PANEL)]
        for i in range(PANEL):
            scale = lax.rsqrt(square[i, i])
            scaled = {k: square[i, k] * scale for k in range(i + 1, PANEL)}
            xs[i], ys[i] = xs[i] * scale, ys[i] * scale
            for k in range(i + 1, PANEL):
                for m in range(k, PANEL):
                    square[k, m] = square[k, m] - scaled[k] * scaled[m]
                xs[k] = xs[k] - scaled[k] * xs[i]
                ys[k] = ys[k] - scaled[k] * ys[i]
        upper, lower = [], []
        for tile in range(0, PANEL, 8):
            u, v = xs[tile], ys[tile]
            for i in range(1, 8):
                u = jnp.where(sub == i, xs[tile + i], u)
                v = jnp.where(sub == i, ys[tile + i], v)
            upper.append(u)
            lower.append(v)
        u, v = jnp.concatenate(upper, axis=0), jnp.concatenate(lower, axis=0)
        right[pl.ds(base, PANEL), :] = v
        rest = size - base - PANEL
        if rest:
            a, b, c = three_parts(jnp.concatenate([u, v], axis=1))
            one = jnp.concatenate([part[:, :size] for part in (a, a, b, a, b, c)], axis=0)
            two = jnp.concatenate([a, b, a, c, b, a], axis=0)
            update = lax.dot_general(
                one, two, (((0,), (0,)), ((), ())), preferred_element_type=jnp.float32
            )[base + PANEL :]
            left[pl.ds(base + PANEL, rest), :] -= update[:, :size]
            right[pl.ds(base + PANEL, rest), :] -= update[:, size:]


def folded(gram):
    lane = lax.broadcasted_iota(jnp.int32, (32, LANES), 1)
    second = jnp.where(lane < 32, pltpu.roll(gram[96:], 32, 1), gram[32:64])
    third = jnp.where(lane[:16] < 64, pltpu.roll(gram[64:80], 64, 1), gram[80:96])
    return jnp.concatenate([gram[:32], second, third], axis=0)


def unfolded(packed):
    third = packed[64:]
    corner = pltpu.roll(packed[32:64], 96, 1)
    return jnp.concatenate([packed[:64], pltpu.roll(third, 64, 1), third, corner], axis=0)


def basis_kernel(plan, scale, addends, *rest):
    own, one, two, three = (ref[...] for ref in rest[:addends])
    packed = (own + one) + (two + three)
    split_ref, out_hbm, left, right, held, sems = rest[addends:]
    invert_factor(unfolded(packed), left, right)
    weight = right[...] * scale
    high = weight.astype(jnp.bfloat16)
    low = (weight - high.astype(jnp.float32)).astype(jnp.bfloat16)
    turned = jnp.concatenate(
        [jnp.concatenate([high, high], axis=1), jnp.concatenate([low, low], axis=1)], axis=0
    )
    copies = []
    for start in range(0, plan.rows, CHUNK):
        size = min(CHUNK, plan.rows - start)
        kept = min(size, plan.segment - start)
        for station in range(plan.band):
            product = lax.dot_general(
                split_ref[station, pl.ds(start, size), :],
                turned,
                (((1,), (1,)), ((), ())),
                preferred_element_type=jnp.float32,
            )
            total = product[:, :LANES] + product[:, LANES:]
            held[pl.ds(start * plan.band + station, size, stride=plan.band), :] = total
        rows = pl.ds(start * plan.band, kept * plan.band)
        copies.append(pltpu.make_async_copy(held.at[rows], out_hbm.at[rows], sems.at[len(copies)]))
        copies[-1].start()
    for copy in copies:
        copy.wait()


def make_basis(plan, scale, grams, split):
    vmem = pl.BlockSpec(memory_space=pltpu.VMEM)
    shape = (plan.segment * plan.band, LANES)
    rows = pl.pallas_call(
        functools.partial(basis_kernel, plan, scale, len(grams)),
        out_shape=jax.ShapeDtypeStruct(shape, jnp.float32),
        in_specs=[vmem] * (len(grams) + 1),
        out_specs=pl.BlockSpec(memory_space=pl.ANY),
        scratch_shapes=[pltpu.VMEM((LANES, LANES), jnp.float32)] * 2
        + [pltpu.VMEM((plan.rows * plan.band, LANES), jnp.float32), pltpu.SemaphoreType.DMA((-(-plan.rows // CHUNK),))],
        compiler_params=pltpu.CompilerParams(vmem_limit_bytes=24 << 20),
        name="factor_and_basis",
    )(*grams, split)
    return rows.reshape(plan.segment, plan.band, LANES).transpose(1, 0, 2)


def sum_four(value, axis, bit):
    one, two, three = (swapped(value, axis, k << bit) for k in (1, 2, 3))
    return (value + one) + (two + three)


def sum_over(value, axis, bits):
    while bits:
        if len(bits) > 1:
            value = sum_four(value, axis, bits[0])
            bits = bits[2:]
        else:
            value = value + swapped(value, axis, 1 << bits[0])
            bits = bits[1:]
    return value


def both_cores(values):
    return values + [swapped(value, "band", 1) for value in values]


def local(probes, kernel, pair_station, pair_count):
    length, probe_count = probes.shape[2:]
    slots, taps = kernel.shape[1], kernel.shape[3]
    band_size, grp_size = lax.axis_size("band"), lax.axis_size("grp")
    plan = Plan(length, taps, slots, band_size)
    band = lax.axis_index("band").astype(jnp.int32).reshape(1)
    messages = pack(
        plan, band, probes.reshape(length, probe_count), kernel.reshape(slots, taps), pair_station, pair_count
    )
    arrived = [
        value if mask == 0 else swapped(value, "band", mask)
        for value, (mask, near) in zip(messages, plan.sends)
    ]
    near = sum(near for _, near in plan.sends)
    field = add_rows(plan, band, both_cores(arrived[:1]), None, False)
    field = add_rows(plan, band, arrived[1 : 1 + near], field, False)
    *head, tail = arrived[1 + near :]
    passed = [swapped(value, "band", 1) for value in head]
    field = add_rows(plan, band, head, field, False)
    tail, field = lax.optimization_barrier((tail, field))
    tail_passed = swapped(tail, "band", 1)
    field = add_rows(plan, band, [tail, *passed], field, False)
    field = add_rows(plan, band, [tail_passed], field, True)
    split, gram = field
    band_bits, grp_bits = (list(range(n.bit_length() - 1)) for n in (band_size, grp_size))
    gram = sum_over(gram, "band", band_bits[:1])
    gram = sum_over(gram, "grp", grp_bits)
    gram = sum_over(gram, "band", band_bits[1:-2])
    grams = [gram] + [swapped(gram, "band", k << band_bits[-2]) for k in (1, 2, 3)]
    scale = float(grp_size * band_size * length) ** 0.5
    return make_basis(plan, scale, grams, split)


def solution(mesh):
    placed = (
        P(("grp", "band"), None, None, None),
        P(("grp", "band"), None, None, None),
        P(("grp", "band"), None),
        P(("grp", "band")),
    )
    return jax.shard_map(
        local, mesh=mesh, in_specs=placed, out_specs=P("grp", "band", None), check_vma=False
    )
```

```python
import functools

import jax
import jax.numpy as jnp
from jax import lax
from jax.experimental import pallas as pl
from jax.experimental.pallas import tpu as pltpu
from jax.sharding import PartitionSpec as P

LANES = 128
TILE = 16
BLOCK = 32
PANEL = 16
CHUNK = 272


def up(value, step):
    return -(-value // step) * step


def swapped(value, axis, mask):
    pairs = [(source, source ^ mask) for source in range(lax.axis_size(axis))]
    return lax.ppermute(value, axis, pairs)


class Plan:
    def __init__(self, length, taps, slots, band_size):
        self.length, self.taps, self.slots, self.band = length, taps, slots, band_size
        self.half = (taps - 1) // 2
        self.segment = length // band_size
        starts = [b * self.segment - self.half for b in range(band_size)]
        self.aligned = [s // TILE * TILE for s in starts]
        self.shifts = [s - a for s, a in zip(starts, self.aligned)]
        self.rows = up(self.segment, TILE)
        blocks = -(-self.segment // BLOCK)
        self.block_starts = [min(i * BLOCK, self.rows - BLOCK) for i in range(blocks)]
        self.depth = up(BLOCK + taps - 1 + max(self.shifts), TILE)
        self.sub = self.block_starts[-1] + self.depth
        self.chip_starts = [self.aligned[b // 2 * 2] for b in range(band_size)]
        self.offsets = [a - c for a, c in zip(self.aligned, self.chip_starts)]
        reach = self.segment + taps - 1
        self.window = up(max(o + s + reach for o, s in zip(self.offsets, self.shifts)), TILE)
        self.left = -min(self.chip_starts)
        self.tap_rows = -(-taps // LANES)
        self.extra = up(slots * self.tap_rows + 1, TILE)
        self.whole = self.window + self.extra
        assert max(self.offsets) + self.sub <= self.whole
        self.near = self.sub + self.extra
        self.sends = [(0, False)] + [(m, True) for m in (2, 3)][: band_size - 2]
        self.sends += [(m, False) for m in range(4, band_size, 2)]

    def size(self, near):
        return self.sub if near else self.window

    def shapes(self, sends):
        return [jax.ShapeDtypeStruct((self.size(near) + self.extra, LANES), jnp.bfloat16) for _, near in sends]


def pack_kernel(plan, sends, band_ref, count_ref, station_hbm, taps_hbm, probes_hbm, *rest):
    peers = len(sends)
    messages = rest[:peers]
    station_ref, taps_ref, rows_f32, in_sems, out_sems = rest[peers:]
    loads = [(station_hbm, station_ref), (taps_hbm, taps_ref)]
    loads = [pltpu.make_async_copy(a, b, in_sems.at[i]) for i, (a, b) in enumerate(loads)]
    for copy in loads:
        copy.start()

    def windows(peer, act):
        mask, near = sends[peer]
        size = plan.size(near)
        other = band_ref[0] ^ mask
        if not near:
            other = other // 2 * 2
        plain = other >= 0
        for index in range(0, plan.band, 1 if near else 2):
            start = plan.aligned[index]
            if start < 0:
                first, cut = plan.length + start, -start
            elif start + size > plan.length:
                first, cut = start, plan.length - start
            else:
                continue
            plain = jnp.logical_and(plain, other != index)

            @pl.when(other == index)
            def _():
                for piece, (low, to, count) in enumerate([(first, 0, cut), (0, cut, size - cut)]):
                    act(
                        pltpu.make_async_copy(
                            probes_hbm.at[pl.ds(low, count)],
                            messages[peer].at[pl.ds(to, count)],
                            out_sems.at[2 * peer + piece],
                        )
                    )

        @pl.when(plain)
        def _():
            low = (other * plan.segment + plan.left - plan.half) // TILE * TILE - plan.left
            act(
                pltpu.make_async_copy(
                    probes_hbm.at[pl.ds(pl.multiple_of(low, TILE), size)],
                    messages[peer].at[pl.ds(0, size)],
                    out_sems.at[2 * peer],
                )
            )

    order = list(range(peers))[::-1]
    for peer in order:
        windows(peer, lambda copy: copy.start())
    rows_f32[...] = jnp.zeros_like(rows_f32)
    for copy in loads:
        copy.wait()
    live = count_ref[0]
    for slot in range(plan.slots):
        keep = (slot < live).astype(jnp.float32)
        for part in range(plan.tap_rows):
            low = part * LANES
            width = min(LANES, plan.taps - low)
            piece = taps_ref[pl.ds(slot, 1), pl.ds(low, width)].astype(jnp.float32)
            rows_f32[pl.ds(slot * plan.tap_rows + part, 1), pl.ds(0, width)] = piece * keep
    lane = lax.broadcasted_iota(jnp.int32, (1, LANES), 1)
    names = jnp.zeros((1, LANES), jnp.float32)
    for slot in range(plan.slots):
        names = jnp.where(lane == slot, station_ref[0, slot].astype(jnp.float32), names)
    rows_f32[pl.ds(plan.slots * plan.tap_rows, 1), :] = names
    rows_bf = rows_f32[...].astype(jnp.bfloat16)
    for peer in order:
        messages[peer][pl.ds(plan.size(sends[peer][1]), plan.extra), :] = rows_bf
    for peer in order:
        windows(peer, lambda copy: copy.wait())


def stay(value):
    return pltpu.with_memory_space_constraint(value, pltpu.HBM)


def pack(plan, sends, band, probes, taps, station, count):
    peers = len(sends)
    hbm = pl.BlockSpec(memory_space=pltpu.HBM)
    smem = pl.BlockSpec(memory_space=pltpu.SMEM)
    return pl.pallas_call(
        functools.partial(pack_kernel, plan, sends),
        out_shape=plan.shapes(sends),
        in_specs=[smem] * 2 + [hbm] * 3,
        out_specs=[pl.BlockSpec(memory_space=pltpu.VMEM)] * peers,
        scratch_shapes=[
            pltpu.SMEM(station.shape, jnp.int32),
            pltpu.VMEM(taps.shape, jnp.bfloat16),
            pltpu.VMEM((plan.extra, LANES), jnp.float32),
            pltpu.SemaphoreType.DMA((2,)),
            pltpu.SemaphoreType.DMA((2 * peers,)),
        ],
        compiler_params=pltpu.CompilerParams(vmem_limit_bytes=8 << 20),
        cost_estimate=pl.CostEstimate(flops=0, bytes_accessed=4 << 20, transcendentals=0),
        name="pack_windows",
    )(band, count, stay(station), stay(taps), stay(probes))


def add_products(plan, place, messages, field, table):
    offset, shift = place
    lanes = up(plan.depth, LANES)
    for source, message in enumerate(messages):
        near = message.shape[0] == plan.near
        source = source % 2
        rows = message[pl.ds(plan.size(near), plan.extra), :].astype(jnp.float32)
        names = rows[plan.slots * plan.tap_rows : plan.slots * plan.tap_rows + 1, :]
        for slot in range(plan.slots):
            pieces = [
                rows[slot * plan.tap_rows + part : slot * plan.tap_rows + part + 1, :]
                for part in range(plan.tap_rows)
            ]
            pieces += [jnp.zeros((1, LANES), jnp.float32)] * (lanes // LANES - plan.tap_rows)
            moved = pltpu.roll(jnp.concatenate(pieces, axis=1), shift, 1)
            spread = jnp.broadcast_to(moved, (BLOCK, lanes))
            rolled = pltpu.roll(spread, 0, 1, stride=1, stride_axis=0)
            table[source, pl.ds(slot * BLOCK, BLOCK), :] = rolled[:, : plan.depth].astype(jnp.bfloat16)
        right = jnp.concatenate(
            [
                message[pl.ds(start if near else pl.multiple_of(offset + start, TILE), plan.depth), :]
                for start in plan.block_starts
            ],
            axis=1,
        )
        products = jnp.dot(table[source], right, preferred_element_type=jnp.float32)
        for slot in range(plan.slots):
            product = products[slot * BLOCK : (slot + 1) * BLOCK]
            station = names[0, slot].astype(jnp.int32)
            done = 0
            for i, start in enumerate(plan.block_starts):
                skip = done - start
                field[station, pl.ds(done, BLOCK - skip), :] += product[
                    skip:, i * LANES : (i + 1) * LANES
                ]
                done = start + BLOCK


def split_and_gram(plan, field, split_ref, gram_ref, total):
    total[...] = jnp.zeros_like(total)
    inside = lax.broadcasted_iota(jnp.int32, (plan.rows, LANES), 0) < plan.segment

    for station in range(plan.band):
        values = jnp.where(inside, field[station], 0.0)
        high = values.astype(jnp.bfloat16)
        low = (values - high.astype(jnp.float32)).astype(jnp.bfloat16)
        both = jnp.concatenate([high, low], axis=1)
        split_ref[station] = both
        total[...] += lax.dot_general(
            both, both, (((0,), (0,)), ((), ())), preferred_element_type=jnp.float32
        )

    rows = total[pl.ds(0, LANES), :] + total[pl.ds(LANES, LANES), :]
    gram_ref[...] = folded(rows[:, :LANES] + rows[:, LANES:])


def field_kernel(plan, first, last, count, band_ref, *rest):
    messages, rest = rest[:count], rest[count:]
    if not first:
        field, rest = rest[0], rest[1:]
    base = band_ref[0] * plan.segment + plan.left - plan.half
    chip = band_ref[0] // 2 * (2 * plan.segment) + plan.left - plan.half
    aligned = base // TILE * TILE
    place = (aligned - chip // TILE * TILE, base - aligned)
    if last:
        split_ref, gram_ref, table, total = rest
        add_products(plan, place, messages, field, table)
        split_and_gram(plan, field, split_ref, gram_ref, total)
    else:
        out_ref, table = rest
        if first:
            out_ref[...] = jnp.zeros_like(out_ref)
        add_products(plan, place, messages, out_ref, table)


def add_rows(plan, band, messages, field, last):
    count, first = len(messages), field is None
    vmem = pl.BlockSpec(memory_space=pltpu.VMEM)
    field_shape = jax.ShapeDtypeStruct((plan.band, plan.rows, LANES), jnp.float32)
    if last:
        out_shape = [
            jax.ShapeDtypeStruct((plan.band, plan.rows, 2 * LANES), jnp.bfloat16),
            jax.ShapeDtypeStruct((LANES * 5 // 8, LANES), jnp.float32),
        ]
    else:
        out_shape = field_shape
    operands = [band, *messages] + ([] if first else [field])
    return pl.pallas_call(
        functools.partial(field_kernel, plan, first, last, count),
        out_shape=out_shape,
        in_specs=[pl.BlockSpec(memory_space=pltpu.SMEM)] + [vmem] * (len(operands) - 1),
        out_specs=[vmem] * 2 if last else vmem,
        input_output_aliases={} if first or last else {len(operands) - 1: 0},
        scratch_shapes=[pltpu.VMEM((min(count, 2), plan.slots * BLOCK, plan.depth), jnp.bfloat16)]
        + ([pltpu.VMEM((2 * LANES, 2 * LANES), jnp.float32)] if last else []),
        compiler_params=pltpu.CompilerParams(vmem_limit_bytes=24 << 20),
        cost_estimate=pl.CostEstimate(flops=1 << 20, bytes_accessed=1 << 16, transcendentals=0),
        name="field_and_gram" if last else "field",
    )(*operands)


def three_parts(value):
    first = value.astype(jnp.bfloat16)
    value = value - first.astype(jnp.float32)
    second = value.astype(jnp.bfloat16)
    return first, second, (value - second.astype(jnp.float32)).astype(jnp.bfloat16)


def invert_factor(gram, left, right):
    size = gram.shape[0]
    row = lax.broadcasted_iota(jnp.int32, (size, size), 0)
    col = lax.broadcasted_iota(jnp.int32, (size, size), 1)
    left[...] = gram
    right[...] = (row == col).astype(jnp.float32)
    sub = lax.broadcasted_iota(jnp.int32, (8, size), 0)
    for base in range(0, size, PANEL):
        x, y = left[pl.ds(base, PANEL), :], right[pl.ds(base, PANEL), :]
        square = {}
        for i in range(PANEL):
            for k in range(i, PANEL):
                square[i, k] = jnp.broadcast_to(x[i : i + 1, base + k : base + k + 1], (8, size))
        xs = [jnp.broadcast_to(x[i : i + 1, :], (8, size)) for i in range(PANEL)]
        ys = [jnp.broadcast_to(y[i : i + 1, :], (8, size)) for i in range(PANEL)]
        for i in range(PANEL):
            scale = lax.rsqrt(square[i, i])
            scaled = {k: square[i, k] * scale for k in range(i + 1, PANEL)}
            xs[i], ys[i] = xs[i] * scale, ys[i] * scale
            for k in range(i + 1, PANEL):
                for m in range(k, PANEL):
                    square[k, m] = square[k, m] - scaled[k] * scaled[m]
                xs[k] = xs[k] - scaled[k] * xs[i]
                ys[k] = ys[k] - scaled[k] * ys[i]
        upper, lower = [], []
        for tile in range(0, PANEL, 8):
            u, v = xs[tile], ys[tile]
            for i in range(1, 8):
                u = jnp.where(sub == i, xs[tile + i], u)
                v = jnp.where(sub == i, ys[tile + i], v)
            upper.append(u)
            lower.append(v)
        u, v = jnp.concatenate(upper, axis=0), jnp.concatenate(lower, axis=0)
        right[pl.ds(base, PANEL), :] = v
        rest = size - base - PANEL
        if rest:
            a, b, c = three_parts(jnp.concatenate([u, v], axis=1))
            one = jnp.concatenate([part[:, :size] for part in (a, a, b, a, b, c)], axis=0)
            two = jnp.concatenate([a, b, a, c, b, a], axis=0)
            update = lax.dot_general(
                one, two, (((0,), (0,)), ((), ())), preferred_element_type=jnp.float32
            )[base + PANEL :]
            left[pl.ds(base + PANEL, rest), :] -= update[:, :size]
            right[pl.ds(base + PANEL, rest), :] -= update[:, size:]


def folded(gram):
    lane = lax.broadcasted_iota(jnp.int32, (32, LANES), 1)
    second = jnp.where(lane < 32, pltpu.roll(gram[96:], 32, 1), gram[32:64])
    third = jnp.where(lane[:16] < 64, pltpu.roll(gram[64:80], 64, 1), gram[80:96])
    return jnp.concatenate([gram[:32], second, third], axis=0)


def unfolded(packed):
    third = packed[64:]
    corner = pltpu.roll(packed[32:64], 96, 1)
    return jnp.concatenate([packed[:64], pltpu.roll(third, 64, 1), third, corner], axis=0)


def basis_kernel(plan, scale, addends, *rest):
    own, one, two, three = (ref[...] for ref in rest[:addends])
    packed = (own + one) + (two + three)
    split_ref, out_hbm, left, right, held, sems = rest[addends:]
    invert_factor(unfolded(packed), left, right)
    weight = right[...] * scale
    high = weight.astype(jnp.bfloat16)
    low = (weight - high.astype(jnp.float32)).astype(jnp.bfloat16)
    turned = jnp.concatenate(
        [jnp.concatenate([high, high], axis=1), jnp.concatenate([low, low], axis=1)], axis=0
    )
    copies = []
    for start in range(0, plan.rows, CHUNK):
        size = min(CHUNK, plan.rows - start)
        kept = min(size, plan.segment - start)
        for station in range(plan.band):
            product = lax.dot_general(
                split_ref[station, pl.ds(start, size), :],
                turned,
                (((1,), (1,)), ((), ())),
                preferred_element_type=jnp.float32,
            )
            total = product[:, :LANES] + product[:, LANES:]
            held[pl.ds(start * plan.band + station, size, stride=plan.band), :] = total
        rows = pl.ds(start * plan.band, kept * plan.band)
        copies.append(pltpu.make_async_copy(held.at[rows], out_hbm.at[rows], sems.at[len(copies)]))
        copies[-1].start()
    for copy in copies:
        copy.wait()


def make_basis(plan, scale, grams, split):
    vmem = pl.BlockSpec(memory_space=pltpu.VMEM)
    shape = (plan.segment * plan.band, LANES)
    rows = pl.pallas_call(
        functools.partial(basis_kernel, plan, scale, len(grams)),
        out_shape=jax.ShapeDtypeStruct(shape, jnp.float32),
        in_specs=[vmem] * (len(grams) + 1),
        out_specs=pl.BlockSpec(memory_space=pl.ANY),
        scratch_shapes=[pltpu.VMEM((LANES, LANES), jnp.float32)] * 2
        + [pltpu.VMEM((plan.rows * plan.band, LANES), jnp.float32), pltpu.SemaphoreType.DMA((-(-plan.rows // CHUNK),))],
        compiler_params=pltpu.CompilerParams(vmem_limit_bytes=24 << 20),
        name="factor_and_basis",
    )(*grams, split)
    return rows.reshape(plan.segment, plan.band, LANES).transpose(1, 0, 2)


def sum_four(value, axis, bit):
    one, two, three = (swapped(value, axis, k << bit) for k in (1, 2, 3))
    return (value + one) + (two + three)


def sum_over(value, axis, bits):
    while bits:
        if len(bits) > 1:
            value = sum_four(value, axis, bits[0])
            bits = bits[2:]
        else:
            value = value + swapped(value, axis, 1 << bits[0])
            bits = bits[1:]
    return value


def both_cores(values):
    return values + [swapped(value, "band", 1) for value in values]


def local(probes, kernel, pair_station, pair_count):
    length, probe_count = probes.shape[2:]
    slots, taps = kernel.shape[1], kernel.shape[3]
    band_size, grp_size = lax.axis_size("band"), lax.axis_size("grp")
    plan = Plan(length, taps, slots, band_size)
    band = lax.axis_index("band").astype(jnp.int32).reshape(1)
    operands = probes.reshape(length, probe_count), kernel.reshape(slots, taps), pair_station, pair_count
    close = [send for send in plan.sends if send[0] < 4]
    messages = pack(plan, plan.sends[len(close) :], band, *operands)
    messages = pack(plan, close, band, *operands) + messages
    arrived = [
        value if mask == 0 else swapped(value, "band", mask)
        for value, (mask, near) in zip(messages, plan.sends)
    ]
    near = sum(near for _, near in plan.sends)
    field = add_rows(plan, band, both_cores(arrived[:1]), None, False)
    field = add_rows(plan, band, arrived[1 : 1 + near], field, False)
    *head, tail = arrived[1 + near :]
    passed = [swapped(value, "band", 1) for value in head]
    field = add_rows(plan, band, head, field, False)
    tail, field = lax.optimization_barrier((tail, field))
    tail_passed = swapped(tail, "band", 1)
    field = add_rows(plan, band, [tail, *passed], field, False)
    field = add_rows(plan, band, [tail_passed], field, True)
    split, gram = field
    band_bits, grp_bits = (list(range(n.bit_length() - 1)) for n in (band_size, grp_size))
    gram = sum_over(gram, "band", band_bits[:1])
    gram = sum_over(gram, "grp", grp_bits)
    gram = sum_over(gram, "band", band_bits[1:-2])
    grams = [gram] + [swapped(gram, "band", k << band_bits[-2]) for k in (1, 2, 3)]
    scale = float(grp_size * band_size * length) ** 0.5
    return make_basis(plan, scale, grams, split)


def solution(mesh):
    placed = (
        P(("grp", "band"), None, None, None),
        P(("grp", "band"), None, None, None),
        P(("grp", "band"), None),
        P(("grp", "band")),
    )
    return jax.shard_map(
        local, mesh=mesh, in_specs=placed, out_specs=P("grp", "band", None), check_vma=False
    )
```

```python
import functools

import jax
import jax.numpy as jnp
from jax import lax
from jax.experimental import pallas as pl
from jax.experimental.pallas import tpu as pltpu
from jax.sharding import PartitionSpec as P

LANES = 128
TILE = 16
BLOCK = 48
PANEL = 16
CHUNK = 272


def up(value, step):
    return -(-value // step) * step


def swapped(value, axis, mask):
    pairs = [(source, source ^ mask) for source in range(lax.axis_size(axis))]
    return lax.ppermute(value, axis, pairs)


class Plan:
    def __init__(self, length, taps, slots, band_size):
        self.length, self.taps, self.slots, self.band = length, taps, slots, band_size
        self.half = (taps - 1) // 2
        self.segment = length // band_size
        starts = [b * self.segment - self.half for b in range(band_size)]
        self.aligned = [s // TILE * TILE for s in starts]
        self.shifts = [s - a for s, a in zip(starts, self.aligned)]
        self.rows = up(self.segment, TILE)
        blocks = -(-self.segment // BLOCK)
        self.block_starts = [min(i * BLOCK, self.rows - BLOCK) for i in range(blocks)]
        self.depth = up(BLOCK + taps - 1 + max(self.shifts), TILE)
        self.sub = self.block_starts[-1] + self.depth
        self.chip_starts = [self.aligned[b // 2 * 2] for b in range(band_size)]
        self.offsets = [a - c for a, c in zip(self.aligned, self.chip_starts)]
        reach = self.segment + taps - 1
        self.window = up(max(o + s + reach for o, s in zip(self.offsets, self.shifts)), TILE)
        self.left = -min(self.chip_starts)
        self.tap_rows = -(-taps // LANES)
        self.extra = up(slots * self.tap_rows + 1, TILE)
        self.whole = self.window + self.extra
        assert max(self.offsets) + self.sub <= self.whole
        self.near = self.sub + self.extra
        self.sends = [(0, False)] + [(m, True) for m in (2, 3)][: band_size - 2]
        self.sends += [(m, False) for m in range(4, band_size, 2)]

    def size(self, near):
        return self.sub if near else self.window

    def shapes(self):
        return [jax.ShapeDtypeStruct((self.size(near) + self.extra, LANES), jnp.bfloat16) for _, near in self.sends]


def pack_kernel(plan, band_ref, count_ref, station_hbm, taps_hbm, probes_hbm, *rest):
    peers = len(plan.sends)
    messages = rest[:peers]
    station_ref, taps_ref, rows_f32, in_sems, out_sems = rest[peers:]
    loads = [(station_hbm, station_ref), (taps_hbm, taps_ref)]
    loads = [pltpu.make_async_copy(a, b, in_sems.at[i]) for i, (a, b) in enumerate(loads)]
    for copy in loads:
        copy.start()

    def windows(peer, act):
        mask, near = plan.sends[peer]
        size = plan.size(near)
        other = band_ref[0] ^ mask
        if not near:
            other = other // 2 * 2
        plain = other >= 0
        for index in range(0, plan.band, 1 if near else 2):
            start = plan.aligned[index]
            if start < 0:
                first, cut = plan.length + start, -start
            elif start + size > plan.length:
                first, cut = start, plan.length - start
            else:
                continue
            plain = jnp.logical_and(plain, other != index)

            @pl.when(other == index)
            def _():
                for piece, (low, to, count) in enumerate([(first, 0, cut), (0, cut, size - cut)]):
                    act(
                        pltpu.make_async_copy(
                            probes_hbm.at[pl.ds(low, count)],
                            messages[peer].at[pl.ds(to, count)],
                            out_sems.at[2 * peer + piece],
                        )
                    )

        @pl.when(plain)
        def _():
            low = (other * plan.segment + plan.left - plan.half) // TILE * TILE - plan.left
            act(
                pltpu.make_async_copy(
                    probes_hbm.at[pl.ds(pl.multiple_of(low, TILE), size)],
                    messages[peer].at[pl.ds(0, size)],
                    out_sems.at[2 * peer],
                )
            )

    order = list(range(peers))[::-1]
    for peer in order:
        windows(peer, lambda copy: copy.start())
    rows_f32[...] = jnp.zeros_like(rows_f32)
    for copy in loads:
        copy.wait()
    live = count_ref[0]
    for slot in range(plan.slots):
        keep = (slot < live).astype(jnp.float32)
        for part in range(plan.tap_rows):
            low = part * LANES
            width = min(LANES, plan.taps - low)
            piece = taps_ref[pl.ds(slot, 1), pl.ds(low, width)].astype(jnp.float32)
            rows_f32[pl.ds(slot * plan.tap_rows + part, 1), pl.ds(0, width)] = piece * keep
    lane = lax.broadcasted_iota(jnp.int32, (1, LANES), 1)
    names = jnp.zeros((1, LANES), jnp.float32)
    for slot in range(plan.slots):
        names = jnp.where(lane == slot, station_ref[0, slot].astype(jnp.float32), names)
    rows_f32[pl.ds(plan.slots * plan.tap_rows, 1), :] = names
    rows_bf = rows_f32[...].astype(jnp.bfloat16)
    for peer in order:
        messages[peer][pl.ds(plan.size(plan.sends[peer][1]), plan.extra), :] = rows_bf
    for peer in order:
        windows(peer, lambda copy: copy.wait())


def stay(value):
    return pltpu.with_memory_space_constraint(value, pltpu.HBM)


def pack(plan, band, probes, taps, station, count):
    peers = len(plan.sends)
    hbm = pl.BlockSpec(memory_space=pltpu.HBM)
    smem = pl.BlockSpec(memory_space=pltpu.SMEM)
    return pl.pallas_call(
        functools.partial(pack_kernel, plan),
        out_shape=plan.shapes(),
        in_specs=[smem] * 2 + [hbm] * 3,
        out_specs=[pl.BlockSpec(memory_space=pltpu.VMEM)] * peers,
        scratch_shapes=[
            pltpu.SMEM(station.shape, jnp.int32),
            pltpu.VMEM(taps.shape, jnp.bfloat16),
            pltpu.VMEM((plan.extra, LANES), jnp.float32),
            pltpu.SemaphoreType.DMA((2,)),
            pltpu.SemaphoreType.DMA((2 * peers,)),
        ],
        compiler_params=pltpu.CompilerParams(vmem_limit_bytes=8 << 20),
        cost_estimate=pl.CostEstimate(flops=0, bytes_accessed=4 << 20, transcendentals=0),
        name="pack_windows",
    )(band, count, stay(station), stay(taps), stay(probes))


def add_products(plan, place, messages, field, table):
    offset, shift = place
    lanes = up(plan.depth, LANES)
    for source, message in enumerate(messages):
        near = message.shape[0] == plan.near
        source = source % 2
        rows = message[pl.ds(plan.size(near), plan.extra), :].astype(jnp.float32)
        names = rows[plan.slots * plan.tap_rows : plan.slots * plan.tap_rows + 1, :]
        for slot in range(plan.slots):
            pieces = [
                rows[slot * plan.tap_rows + part : slot * plan.tap_rows + part + 1, :]
                for part in range(plan.tap_rows)
            ]
            pieces += [jnp.zeros((1, LANES), jnp.float32)] * (lanes // LANES - plan.tap_rows)
            moved = pltpu.roll(jnp.concatenate(pieces, axis=1), shift, 1)
            spread = jnp.broadcast_to(moved, (BLOCK, lanes))
            rolled = pltpu.roll(spread, 0, 1, stride=1, stride_axis=0)
            table[source, pl.ds(slot * BLOCK, BLOCK), :] = rolled[:, : plan.depth].astype(jnp.bfloat16)
        right = jnp.concatenate(
            [
                message[pl.ds(start if near else pl.multiple_of(offset + start, TILE), plan.depth), :]
                for start in plan.block_starts
            ],
            axis=1,
        )
        products = jnp.dot(table[source], right, preferred_element_type=jnp.float32)
        for slot in range(plan.slots):
            product = products[slot * BLOCK : (slot + 1) * BLOCK]
            station = names[0, slot].astype(jnp.int32)
            done = 0
            for i, start in enumerate(plan.block_starts):
                skip = done - start
                field[station, pl.ds(done, BLOCK - skip), :] += product[
                    skip:, i * LANES : (i + 1) * LANES
                ]
                done = start + BLOCK


def split_and_gram(plan, field, split_ref, gram_ref, total):
    total[...] = jnp.zeros_like(total)
    inside = lax.broadcasted_iota(jnp.int32, (plan.rows, LANES), 0) < plan.segment

    for station in range(plan.band):
        values = jnp.where(inside, field[station], 0.0)
        high = values.astype(jnp.bfloat16)
        low = (values - high.astype(jnp.float32)).astype(jnp.bfloat16)
        both = jnp.concatenate([high, low], axis=1)
        split_ref[station] = both
        total[...] += lax.dot_general(
            both, both, (((0,), (0,)), ((), ())), preferred_element_type=jnp.float32
        )

    rows = total[pl.ds(0, LANES), :] + total[pl.ds(LANES, LANES), :]
    gram_ref[...] = folded(rows[:, :LANES] + rows[:, LANES:])


def field_kernel(plan, first, last, count, band_ref, *rest):
    messages, rest = rest[:count], rest[count:]
    if not first:
        field, rest = rest[0], rest[1:]
    base = band_ref[0] * plan.segment + plan.left - plan.half
    chip = band_ref[0] // 2 * (2 * plan.segment) + plan.left - plan.half
    aligned = base // TILE * TILE
    place = (aligned - chip // TILE * TILE, base - aligned)
    if last:
        split_ref, gram_ref, table, total = rest
        add_products(plan, place, messages, field, table)
        split_and_gram(plan, field, split_ref, gram_ref, total)
    else:
        out_ref, table = rest
        if first:
            out_ref[...] = jnp.zeros_like(out_ref)
        add_products(plan, place, messages, out_ref, table)


def add_rows(plan, band, messages, field, last):
    count, first = len(messages), field is None
    vmem = pl.BlockSpec(memory_space=pltpu.VMEM)
    field_shape = jax.ShapeDtypeStruct((plan.band, plan.rows, LANES), jnp.float32)
    if last:
        out_shape = [
            jax.ShapeDtypeStruct((plan.band, plan.rows, 2 * LANES), jnp.bfloat16),
            jax.ShapeDtypeStruct((LANES * 5 // 8, LANES), jnp.float32),
        ]
    else:
        out_shape = field_shape
    operands = [band, *messages] + ([] if first else [field])
    return pl.pallas_call(
        functools.partial(field_kernel, plan, first, last, count),
        out_shape=out_shape,
        in_specs=[pl.BlockSpec(memory_space=pltpu.SMEM)] + [vmem] * (len(operands) - 1),
        out_specs=[vmem] * 2 if last else vmem,
        input_output_aliases={} if first or last else {len(operands) - 1: 0},
        scratch_shapes=[pltpu.VMEM((min(count, 2), plan.slots * BLOCK, plan.depth), jnp.bfloat16)]
        + ([pltpu.VMEM((2 * LANES, 2 * LANES), jnp.float32)] if last else []),
        compiler_params=pltpu.CompilerParams(vmem_limit_bytes=24 << 20),
        cost_estimate=pl.CostEstimate(flops=1 << 20, bytes_accessed=1 << 16, transcendentals=0),
        name="field_and_gram" if last else "field",
    )(*operands)


def three_parts(value):
    first = value.astype(jnp.bfloat16)
    value = value - first.astype(jnp.float32)
    second = value.astype(jnp.bfloat16)
    return first, second, (value - second.astype(jnp.float32)).astype(jnp.bfloat16)


def invert_factor(gram, left, right):
    size = gram.shape[0]
    row = lax.broadcasted_iota(jnp.int32, (size, size), 0)
    col = lax.broadcasted_iota(jnp.int32, (size, size), 1)
    left[...] = gram
    right[...] = (row == col).astype(jnp.float32)
    sub = lax.broadcasted_iota(jnp.int32, (8, size), 0)
    for base in range(0, size, PANEL):
        x, y = left[pl.ds(base, PANEL), :], right[pl.ds(base, PANEL), :]
        square = {}
        for i in range(PANEL):
            for k in range(i, PANEL):
                square[i, k] = jnp.broadcast_to(x[i : i + 1, base + k : base + k + 1], (8, size))
        xs = [jnp.broadcast_to(x[i : i + 1, :], (8, size)) for i in range(PANEL)]
        ys = [jnp.broadcast_to(y[i : i + 1, :], (8, size)) for i in range(PANEL)]
        for i in range(PANEL):
            scale = lax.rsqrt(square[i, i])
            scaled = {k: square[i, k] * scale for k in range(i + 1, PANEL)}
            xs[i], ys[i] = xs[i] * scale, ys[i] * scale
            for k in range(i + 1, PANEL):
                for m in range(k, PANEL):
                    square[k, m] = square[k, m] - scaled[k] * scaled[m]
                xs[k] = xs[k] - scaled[k] * xs[i]
                ys[k] = ys[k] - scaled[k] * ys[i]
        upper, lower = [], []
        for tile in range(0, PANEL, 8):
            u, v = xs[tile], ys[tile]
            for i in range(1, 8):
                u = jnp.where(sub == i, xs[tile + i], u)
                v = jnp.where(sub == i, ys[tile + i], v)
            upper.append(u)
            lower.append(v)
        u, v = jnp.concatenate(upper, axis=0), jnp.concatenate(lower, axis=0)
        right[pl.ds(base, PANEL), :] = v
        rest = size - base - PANEL
        if rest:
            a, b, c = three_parts(jnp.concatenate([u, v], axis=1))
            one = jnp.concatenate([part[:, :size] for part in (a, a, b, a, b, c)], axis=0)
            two = jnp.concatenate([a, b, a, c, b, a], axis=0)
            update = lax.dot_general(
                one, two, (((0,), (0,)), ((), ())), preferred_element_type=jnp.float32
            )[base + PANEL :]
            left[pl.ds(base + PANEL, rest), :] -= update[:, :size]
            right[pl.ds(base + PANEL, rest), :] -= update[:, size:]


def folded(gram):
    lane = lax.broadcasted_iota(jnp.int32, (32, LANES), 1)
    second = jnp.where(lane < 32, pltpu.roll(gram[96:], 32, 1), gram[32:64])
    third = jnp.where(lane[:16] < 64, pltpu.roll(gram[64:80], 64, 1), gram[80:96])
    return jnp.concatenate([gram[:32], second, third], axis=0)


def unfolded(packed):
    third = packed[64:]
    corner = pltpu.roll(packed[32:64], 96, 1)
    return jnp.concatenate([packed[:64], pltpu.roll(third, 64, 1), third, corner], axis=0)


def basis_kernel(plan, scale, addends, *rest):
    own, one, two, three = (ref[...] for ref in rest[:addends])
    packed = (own + one) + (two + three)
    split_ref, out_hbm, left, right, held, sems = rest[addends:]
    invert_factor(unfolded(packed), left, right)
    weight = right[...] * scale
    high = weight.astype(jnp.bfloat16)
    low = (weight - high.astype(jnp.float32)).astype(jnp.bfloat16)
    turned = jnp.concatenate(
        [jnp.concatenate([high, high], axis=1), jnp.concatenate([low, low], axis=1)], axis=0
    )
    copies = []
    for start in range(0, plan.rows, CHUNK):
        size = min(CHUNK, plan.rows - start)
        kept = min(size, plan.segment - start)
        for station in range(plan.band):
            product = lax.dot_general(
                split_ref[station, pl.ds(start, size), :],
                turned,
                (((1,), (1,)), ((), ())),
                preferred_element_type=jnp.float32,
            )
            total = product[:, :LANES] + product[:, LANES:]
            held[pl.ds(start * plan.band + station, size, stride=plan.band), :] = total
        rows = pl.ds(start * plan.band, kept * plan.band)
        copies.append(pltpu.make_async_copy(held.at[rows], out_hbm.at[rows], sems.at[len(copies)]))
        copies[-1].start()
    for copy in copies:
        copy.wait()


def make_basis(plan, scale, grams, split):
    vmem = pl.BlockSpec(memory_space=pltpu.VMEM)
    shape = (plan.segment * plan.band, LANES)
    rows = pl.pallas_call(
        functools.partial(basis_kernel, plan, scale, len(grams)),
        out_shape=jax.ShapeDtypeStruct(shape, jnp.float32),
        in_specs=[vmem] * (len(grams) + 1),
        out_specs=pl.BlockSpec(memory_space=pl.ANY),
        scratch_shapes=[pltpu.VMEM((LANES, LANES), jnp.float32)] * 2
        + [pltpu.VMEM((plan.rows * plan.band, LANES), jnp.float32), pltpu.SemaphoreType.DMA((-(-plan.rows // CHUNK),))],
        compiler_params=pltpu.CompilerParams(vmem_limit_bytes=24 << 20),
        name="factor_and_basis",
    )(*grams, split)
    return rows.reshape(plan.segment, plan.band, LANES).transpose(1, 0, 2)


def sum_four(value, axis, bit):
    one, two, three = (swapped(value, axis, k << bit) for k in (1, 2, 3))
    return (value + one) + (two + three)


def sum_over(value, axis, bits):
    while bits:
        if len(bits) > 1:
            value = sum_four(value, axis, bits[0])
            bits = bits[2:]
        else:
            value = value + swapped(value, axis, 1 << bits[0])
            bits = bits[1:]
    return value


def both_cores(values):
    return values + [swapped(value, "band", 1) for value in values]


def local(probes, kernel, pair_station, pair_count):
    length, probe_count = probes.shape[2:]
    slots, taps = kernel.shape[1], kernel.shape[3]
    band_size, grp_size = lax.axis_size("band"), lax.axis_size("grp")
    plan = Plan(length, taps, slots, band_size)
    band = lax.axis_index("band").astype(jnp.int32).reshape(1)
    messages = pack(
        plan, band, probes.reshape(length, probe_count), kernel.reshape(slots, taps), pair_station, pair_count
    )
    arrived = [
        value if mask == 0 else swapped(value, "band", mask)
        for value, (mask, near) in zip(messages, plan.sends)
    ]
    near = sum(near for _, near in plan.sends)
    field = add_rows(plan, band, both_cores(arrived[:1]), None, False)
    field = add_rows(plan, band, arrived[1 : 1 + near], field, False)
    *head, tail = arrived[1 + near :]
    passed = [swapped(value, "band", 1) for value in head]
    field = add_rows(plan, band, head, field, False)
    tail, field = lax.optimization_barrier((tail, field))
    tail_passed = swapped(tail, "band", 1)
    field = add_rows(plan, band, [tail, *passed], field, False)
    field = add_rows(plan, band, [tail_passed], field, True)
    split, gram = field
    band_bits, grp_bits = (list(range(n.bit_length() - 1)) for n in (band_size, grp_size))
    gram = sum_over(gram, "band", band_bits[:1])
    gram = sum_over(gram, "grp", grp_bits)
    gram = sum_over(gram, "band", band_bits[1:-2])
    grams = [gram] + [swapped(gram, "band", k << band_bits[-2]) for k in (1, 2, 3)]
    scale = float(grp_size * band_size * length) ** 0.5
    return make_basis(plan, scale, grams, split)


def solution(mesh):
    placed = (
        P(("grp", "band"), None, None, None),
        P(("grp", "band"), None, None, None),
        P(("grp", "band"), None),
        P(("grp", "band")),
    )
    return jax.shard_map(
        local, mesh=mesh, in_specs=placed, out_specs=P("grp", "band", None), check_vma=False
    )
```
